32 devices in a mesh: rep: 2 (over x), lat: 16 (over z, y, core).
Axes of the slice: x: 2, y: 2, z: 4, core: 2. Of those that a mesh axis runs over, the one named last changes fastest.
Arguments:
- ocean_state: bfloat16 [128, 64, 2160], P(None, ('rep', 'lat')), parts along dimension 1, may hold values from -6 to 6
- cotangent: bfloat16 [128, 64, 2160], P(None, ('rep', 'lat')), parts along dimension 1, may hold values from -6 to 6
- land_mask: int32 [32, 2160], P('lat'), may hold values 0 or 1
- fold_partner: int32 [2160], replicated, may hold values from 0 to 2159, each once
- conv_first: bfloat16 [9, 128, 128], replicated, may hold values from -0.1875 to 0.1875
- conv_second: bfloat16 [9, 128, 128], replicated, may hold values from -0.1875 to 0.1875
Outputs:
- updated: bfloat16 [128, 64, 2160], P(None, ('rep', 'lat')), parts along dimension 1
- grad_state: bfloat16 [128, 64, 2160], P(None, ('rep', 'lat')), parts along dimension 1
- grad_first: float32 [2304, 128], P(('rep', 'lat')), parts along dimension 0
- grad_second: float32 [2304, 128], P(('rep', 'lat')), parts along dimension 0
The draws below stay inside these ranges and needn't reach their ends.
There are 2 independent parts, one for each index of `rep`. The reference program is written for one: setup_inputs(seed, part) draws one part's arguments, and reference() takes and returns one part's arrays. A program takes and returns all parts, laid end to end along the dimension named above; an argument that names none is the same for every part. Nothing has to cross between parts.
Inputs may be any that keep to these rules, and one draw needn't show every extreme that they name: `fold_partner`: each column appears exactly once.
All inputs are finite; a program needn't handle non-finite values. No bound on the sum of `land_mask` on one device may be relied on, other than what follows from the above.
Results may differ from the reference program's by a relative error of at most 0.0032.
Values may be sent and summed in bfloat16 or wider, within the bound.
No kernel may reach another device: no remote copies, remote signals or barrier semaphores. Data moves between devices by JAX's collectives and lax.ppermute only.
A program may use at most 64 MiB of HBM per device.

```python
import jax
import jax.numpy as jnp

C = 128
TAPS = 9
NLON = 2160
NLAT = 32


def touch_ends(entries, key, smallest, largest):
    dims = entries.shape
    place = [jax.random.randint(jax.random.fold_in(key, axis), (), 0, dims[axis]) for axis in range(len(dims))]
    entries = entries.at[tuple(place)].set(smallest)
    longest = dims.index(max(dims))
    place[longest] = (place[longest] + 1) % dims[longest]
    return entries.at[tuple(place)].set(largest)


def levels(rng, dims, pieces, least, top_value):
    gain = 1.0
    for dim, blocks in pieces:
        draws = jax.random.uniform(jax.random.fold_in(jax.random.fold_in(rng, 6), dim), (blocks,), jnp.float32, least / len(pieces), top_value / len(pieces))
        gain = gain * jnp.repeat(jnp.exp(draws), dims[dim] // blocks).reshape((-1,) + (1,) * (len(dims) - 1 - dim))
    return gain


def bell_draw(stream_key, shape, spread, bound, cuts=(), dtype=jnp.bfloat16):
    gain = levels(stream_key, shape, cuts, -0.22, 0.18) if cuts else 1.0
    values = jax.random.normal(stream_key, shape, jnp.float32) * spread * gain
    return jnp.minimum(jnp.maximum(values, -bound), bound).astype(dtype)


def setup_inputs(seed: int = 0, part: int = 0) -> dict:
    splits = jax.random.split(jax.random.key(seed), 7)
    part_splits = jax.random.split(jax.random.fold_in(splits[6], part), 7)
    return {
        "ocean_state": bell_draw(part_splits[0], (C, NLAT, NLON), 1.0, 6.0, ((1, 16),)),
        "cotangent": bell_draw(part_splits[1], (C, NLAT, NLON), 1.0, 6.0, ((1, 16),)),
        "land_mask": touch_ends((jax.random.randint(splits[2], (NLAT, NLON), 0, 3) < 2).astype(jnp.int32), jax.random.fold_in(splits[2], 1), 0, 1),
        "fold_partner": jax.random.permutation(splits[3], NLON).astype(jnp.int32),
        "conv_first": bell_draw(splits[4], (TAPS, C, C), (TAPS * C) ** -0.5, 0.1875),
        "conv_second": bell_draw(splits[5], (TAPS, C, C), (TAPS * C) ** -0.5, 0.1875),
    }


def conv_apply(extended, weights, row_count):
    total = jnp.zeros((weights.shape[1], row_count, extended.shape[2]), jnp.float32)
    for col_tap in range(3):
        rolled = jnp.roll(extended, 1 - col_tap, axis=2).astype(jnp.float32)
        for row_tap in range(3):
            kernel = weights[3 * row_tap + col_tap].astype(jnp.float32)
            total = total + jnp.einsum('oi,irl->orl', kernel, rolled[:, row_tap:row_tap + row_count])
    return total

def conv_adjoint(extended, weights, row_count):
    total = jnp.zeros((weights.shape[2], row_count, extended.shape[2]), jnp.float32)
    for col_tap in range(3):
        rolled = jnp.roll(extended, col_tap - 1, axis=2).astype(jnp.float32)
        for row_tap in range(3):
            kernel = weights[3 * row_tap + col_tap].astype(jnp.float32)
            total = total + jnp.einsum('oi,orl->irl', kernel, rolled[:, 2 - row_tap:2 - row_tap + row_count])
    return total

def fold_term(top_row, weights):
    total = jnp.zeros((weights.shape[2], top_row.shape[1]), jnp.float32)
    for col_tap in range(3):
        kernel = weights[6 + col_tap].astype(jnp.float32)
        total = total + jnp.einsum('oi,ol->il', kernel, jnp.roll(top_row, col_tap - 1, axis=1).astype(jnp.float32))
    return total

def kernel_grad(upstream, extended, row_count):
    parts = [None] * 9
    for col_tap in range(3):
        rolled = jnp.roll(extended, 1 - col_tap, axis=2).astype(jnp.float32)
        for row_tap in range(3):
            parts[3 * row_tap + col_tap] = jnp.einsum('orl,irl->oi', upstream.astype(jnp.float32), rolled[:, row_tap:row_tap + row_count])
    stacked = jnp.stack(parts, 0)
    return stacked.reshape(9 * stacked.shape[1], stacked.shape[2])

def reference(ocean_state, cotangent, land_mask, fold_partner, conv_first, conv_second):
    row_count = ocean_state.shape[1]
    width = ocean_state.shape[0]
    zero_row = jnp.zeros((width, 1, ocean_state.shape[2]), jnp.bfloat16)

    def extend(field):
        folded = field[:, -1, :][:, fold_partner]
        return jnp.concatenate([zero_row, field, folded[:, None, :]], axis=1)
    mask_float = land_mask.astype(jnp.float32)
    ext_state = extend(ocean_state)
    pre = conv_apply(ext_state, conv_first, row_count)
    act = (mask_float * jax.nn.gelu(pre)).astype(jnp.bfloat16)
    ext_act = extend(act)
    updated = (mask_float * (ocean_state.astype(jnp.float32) + conv_apply(ext_act, conv_second, row_count))).astype(jnp.bfloat16)
    gout = cotangent * land_mask.astype(jnp.bfloat16)
    ext_gout = jnp.concatenate([zero_row, gout, zero_row], axis=1)
    dact = conv_adjoint(ext_gout, conv_second, row_count)
    dact = dact.at[:, -1, fold_partner].add(fold_term(gout[:, -1, :], conv_second))
    unused, gelu_back = jax.vjp(jax.nn.gelu, pre)
    dpre = gelu_back(dact * mask_float)[0].astype(jnp.bfloat16)
    ext_dpre = jnp.concatenate([zero_row, dpre, zero_row], axis=1)
    dstate = conv_adjoint(ext_dpre, conv_first, row_count)
    dstate = dstate.at[:, -1, fold_partner].add(fold_term(dpre[:, -1, :], conv_first))
    grad_state = (gout.astype(jnp.float32) + dstate).astype(jnp.bfloat16)
    grad_second = kernel_grad(gout, ext_act, row_count)
    grad_first = kernel_grad(dpre, ext_state, row_count)
    return (updated, grad_state, grad_first, grad_second)
```

```python
import functools

import jax
import jax.numpy as jnp
import numpy as np
from jax import lax
from jax.experimental import pallas as pl
from jax.experimental.pallas import tpu as pltpu
from jax.sharding import PartitionSpec as P

C = 128
F32 = jnp.float32
BF16 = jnp.bfloat16
VMEM = pl.BlockSpec(memory_space=pltpu.VMEM)
SMEM = pl.BlockSpec(memory_space=pltpu.SMEM)
MiB = 1 << 20
OUT, INN = 0, 1
OWN, HALO = 0, 3 * 2 * C
CONTRACT_LAST = (((1,), (1,)), ((), ()))
CONTRACT_ROWS = (((0,), (0,)), ((), ()))


def chunk_of(n):
    for size in (432, 400, 384, 320, 256, 240, 144, 128, 80, 64, 48, 32, 16):
        if n % size == 0:
            return size
    return n


def put_taps(dst, base, slot, row, adjoint):
    n = row.shape[0]
    wide = row.astype(F32)
    before = pltpu.roll(wide, 1, 0).astype(BF16)
    after = pltpu.roll(wide, n - 1, 0).astype(BF16)
    taps = (after, row, before) if adjoint else (before, row, after)
    for b, tap in enumerate(taps):
        at = base + 2 * C * b + C * slot
        dst[:, at : at + C] = tap


def row_tap(a, parity):
    return a + parity * (2 - 2 * a)


def build_forward(dst, w, parity):
    dst[...] = jnp.zeros_like(dst)
    for b in range(3):
        for ro, base, ri, a in (
            (OUT, OWN, OUT, 1), (OUT, OWN, INN, 2), (INN, OWN, OUT, 0), (INN, OWN, INN, 1),
            (OUT, HALO, OUT, 0), (INN, HALO, INN, 2),
        ):
            at = base + 2 * C * b + C * ri
            dst[ro * C : ro * C + C, at : at + C] = w[3 * row_tap(a, parity) + b]


def build_adjoint(dst, w, parity, top):
    dst[...] = jnp.zeros_like(dst)
    for b in range(3):
        for base, r, rin, a in (
            (OWN, OUT, OUT, 1), (OWN, OUT, INN, 2), (OWN, INN, OUT, 0), (OWN, INN, INN, 1),
            (HALO, OUT, OUT, 2 - 2 * top), (HALO, INN, INN, 0),
        ):
            at = base + 2 * C * b + C * r
            dst[at : at + C, rin * C : rin * C + C] = w[3 * row_tap(a, parity) + b]


def fill_forward(dst, own_o, own_i, halo_o, halo_i, fold, top):
    put_taps(dst, OWN, OUT, own_o, False)
    put_taps(dst, OWN, INN, own_i, False)
    put_taps(dst, HALO, INN, halo_i, False)

    @pl.when(top == 0)
    def _():
        put_taps(dst, HALO, OUT, halo_o[...], False)

    @pl.when(top != 0)
    def _():
        put_taps(dst, HALO, OUT, fold[...], False)


def fill_adjoint(dst, own_o, own_i, halo_o, halo_i, spread, top):
    put_taps(dst, OWN, OUT, own_o, True)
    put_taps(dst, OWN, INN, own_i, True)
    put_taps(dst, HALO, INN, halo_i, True)

    @pl.when(top == 0)
    def _():
        put_taps(dst, HALO, OUT, halo_o[...], True)

    @pl.when(top != 0)
    def _():
        for b in range(3):
            at = HALO + 2 * C * b
            dst[:, at : at + C] = spread[:, b * C : b * C + C]


def fold_kernel(flags, partner, outer, fold, spread, src, dst, wide, wide_dst):
    n = fold.shape[0]

    @pl.when(flags[1] != 0)
    def _():
        src[...] = outer[0].astype(F32)
        u = outer[1].astype(F32)
        wide[:, 0:C] = pltpu.roll(u, n - 1, 0)
        wide[:, C : 2 * C] = u
        wide[:, 2 * C :] = pltpu.roll(u, 1, 0)

        def step(i, carry):
            for k in range(8):
                j = i * 8 + k
                at = partner[j]
                dst[pl.ds(j, 1), :] = src[pl.ds(at, 1), :]
                wide_dst[pl.ds(at, 1), :] = wide[pl.ds(j, 1), :]
            return carry

        lax.fori_loop(0, n // 8, step, 0)
        fold[...] = dst[...].astype(BF16)
        spread[...] = wide_dst[...].astype(BF16)


def first_kernel(flags, outer, inner, halo_o, halo_i, fold, spread, mask, w1, w2, outer2, inner2, taps, utaps, fw, ad):
    parity, top = flags[0], flags[1]
    n = fold.shape[0]
    build_forward(fw, w1, parity)
    build_adjoint(ad, w2, parity, top)
    fill_forward(taps, outer[0], inner[0], halo_o.at[0], halo_i[0], fold, top)
    fill_adjoint(utaps, outer[1], inner[1], halo_o.at[1], halo_i[1], spread, top)
    m = chunk_of(n)
    scale = np.float32(np.sqrt(2 / np.pi))

    def step(k, carry):
        rows = pl.ds(pl.multiple_of(k * m, m), m)
        pre = lax.dot_general(taps[rows, :], fw[...], CONTRACT_LAST, preferred_element_type=F32)
        dact = jnp.dot(utaps[rows, :], ad[...], preferred_element_type=F32)
        for slot, row, ref in ((OUT, parity, outer2), (INN, 1 - parity, inner2)):
            x = pre[:, slot * C : slot * C + C]
            d = dact[:, slot * C : slot * C + C]
            keep = mask[row, rows, :].astype(F32)
            square = x * x
            t = jnp.tanh(scale * (x + np.float32(0.044715) * (x * square)))
            cdf = np.float32(0.5) * (1.0 + t)
            slope = cdf + (np.float32(0.5) * x) * (1.0 - t * t) * (scale * (1.0 + np.float32(3 * 0.044715) * square))
            ref[0, rows, :] = (keep * (x * cdf)).astype(BF16)
            ref[1, rows, :] = (slope * (keep * d)).astype(BF16)
        return carry

    lax.fori_loop(0, n // m, step, 0)


def weights_kernel(flags, outer2, inner2, taps, utaps, g1, g2):
    parity, top = flags[0], flags[1]
    act = jnp.concatenate([outer2[0], inner2[0]], axis=1)
    dpre = jnp.concatenate([outer2[1], inner2[1]], axis=1)
    for b in range(3):
        own = slice(OWN + 2 * C * b, OWN + 2 * C * b + 2 * C)
        halo = slice(HALO + 2 * C * b, HALO + 2 * C * b + 2 * C)
        p = lax.dot_general(dpre, taps[:, own], CONTRACT_ROWS, preferred_element_type=F32)
        q = lax.dot_general(dpre, taps[:, halo], CONTRACT_ROWS, preferred_element_type=F32)
        g1[3 * row_tap(0, parity) + b] = p[C:, :C] + q[:C, :C]
        g1[3 + b] = p[:C, :C] + p[C:, C:]
        g1[3 * row_tap(2, parity) + b] = p[:C, C:] + q[C:, C:]
        p = lax.dot_general(utaps[:, own], act, CONTRACT_ROWS, preferred_element_type=F32)
        q = lax.dot_general(utaps[:, halo], act, CONTRACT_ROWS, preferred_element_type=F32)
        edge = q[:C, :C]
        is_top = jnp.full((C, C), top, jnp.int32) != 0
        g2[3 * row_tap(0, parity) + b] = p[C:, :C] + q[C:, C:] + jnp.where(is_top, edge, 0.0)
        g2[3 + b] = p[:C, :C] + p[C:, C:]
        g2[3 * row_tap(2, parity) + b] = p[:C, C:] + jnp.where(is_top, 0.0, edge)


def last_kernel(
    flags, outer, inner, outer2, inner2, halo_o, halo_i, fold, spread, mask, w1, w2, updated, grad, taps, utaps, fw, ad
):
    parity, top = flags[0], flags[1]
    n = fold.shape[0]
    build_forward(fw, w2, parity)
    build_adjoint(ad, w1, parity, top)
    fill_forward(taps, outer2[0], inner2[0], halo_o.at[0], halo_i[0], fold, top)
    fill_adjoint(utaps, outer2[1], inner2[1], halo_o.at[1], halo_i[1], spread, top)
    m = chunk_of(n)

    def step(k, carry):
        rows = pl.ds(pl.multiple_of(k * m, m), m)
        y = lax.dot_general(taps[rows, :], fw[...], CONTRACT_LAST, preferred_element_type=F32)
        d = jnp.dot(utaps[rows, :], ad[...], preferred_element_type=F32)
        for slot, row, ref in ((OUT, parity, outer), (INN, 1 - parity, inner)):
            keep = mask[row, rows, :].astype(F32)
            lanes = slice(slot * C, slot * C + C)
            updated[row, rows, :] = (keep * (ref[0, rows, :].astype(F32) + y[:, lanes])).astype(BF16)
            grad[row, rows, :] = (ref[1, rows, :].astype(F32) + d[:, lanes]).astype(BF16)
        return carry

    lax.fori_loop(0, n // m, step, 0)


def call(kernel, specs, outs, scratch, limit, flops, name):
    return pl.pallas_call(
        kernel,
        in_specs=specs,
        out_specs=tuple(VMEM for _ in outs),
        out_shape=tuple(outs),
        scratch_shapes=scratch,
        compiler_params=pltpu.CompilerParams(vmem_limit_bytes=limit * MiB),
        cost_estimate=pl.CostEstimate(flops=flops, transcendentals=0, bytes_accessed=8 * MiB),
        name=name,
    )


def swap(x, n, inner):
    if inner:
        pairs = [(i, i ^ 1) for i in range(n)]
    else:
        pairs = [(i, i + 1) for i in range(1, n - 1, 2)]
        pairs = pairs + [(j, i) for i, j in pairs]
    return lax.ppermute(x, "lat", pairs)


def scatter_sum(g, n, index):
    bits = n.bit_length() - 1
    order = [0] + list(range(2, bits)) + ([1] if bits > 1 else [])
    g = g.reshape((2,) * bits + g.shape[1:])
    left = list(range(bits - 1, -1, -1))
    for bit in order:
        axis = left.index(bit)
        left.pop(axis)
        mine = (index >> bit) & 1
        keep = lax.dynamic_index_in_dim(g, mine, axis, keepdims=False)
        give = lax.dynamic_index_in_dim(g, 1 - mine, axis, keepdims=False)
        g = keep + lax.ppermute(give, "lat", [(i, i ^ (1 << bit)) for i in range(n)])
    return g


def on_device(ocean_state, cotangent, land_mask, fold_partner, conv_first, conv_second):
    lat = lax.axis_size("lat")
    index = lax.axis_index("lat")
    n = ocean_state.shape[2]
    assert ocean_state.shape[1] == 2 and lat % 2 == 0
    parity = index & 1
    flags = jnp.stack([parity, (index == lat - 1).astype(jnp.int32)]).astype(jnp.int32)
    state = ocean_state.transpose(1, 2, 0)
    mask = jnp.broadcast_to(land_mask.astype(BF16)[:, :, None], state.shape)
    gout = cotangent.transpose(1, 2, 0) * mask

    def pick(row):
        return jnp.stack([lax.dynamic_index_in_dim(v, row, 0, keepdims=False) for v in (state, gout)])

    outer, inner = pick(parity), pick(1 - parity)
    halo_o, halo_i = swap(outer, lat, False), swap(inner, lat, True)

    pair = jax.ShapeDtypeStruct((2, n, C), BF16)
    tapshape = jax.ShapeDtypeStruct((n, 12 * C), BF16)
    row = jax.ShapeDtypeStruct((n, C), BF16)
    row3 = jax.ShapeDtypeStruct((n, 3 * C), BF16)
    grads = jax.ShapeDtypeStruct((9, C, C), F32)
    conv_flops = 2 * 2 * n * C * C * 9 * 2
    fold = call(
        fold_kernel, [SMEM, SMEM, VMEM], [row, row3],
        [pltpu.VMEM((n, C), F32), pltpu.VMEM((n, C), F32), pltpu.VMEM((n, 3 * C), F32), pltpu.VMEM((n, 3 * C), F32)],
        32, conv_flops, "fold",
    )
    big = [pltpu.VMEM((2 * C, 12 * C), BF16), pltpu.VMEM((12 * C, 2 * C), BF16)]

    fold1, spread1 = fold(flags, fold_partner, outer)
    outer2, inner2, taps, utaps = call(
        first_kernel, [SMEM] + [VMEM] * 9, [pair, pair, tapshape, tapshape], big, 56, conv_flops, "first"
    )(flags, outer, inner, halo_o, halo_i, fold1, spread1, mask, conv_first, conv_second)
    halo_o2, halo_i2 = swap(outer2, lat, False), swap(inner2, lat, True)
    g1, g2 = call(
        weights_kernel, [SMEM] + [VMEM] * 4, [grads, grads], [], 56, conv_flops, "wgrad"
    )(flags, outer2, inner2, taps, utaps)
    fold2, spread2 = fold(flags, fold_partner, outer2)
    per = 9 * C // lat
    g = jnp.stack([g1.reshape(lat, per, C), g2.reshape(lat, per, C)], axis=1)
    g = scatter_sum(g, lat, index)
    updated, grad = call(
        last_kernel, [SMEM] + [VMEM] * 11, [pair, pair],
        [pltpu.VMEM((n, 12 * C), BF16), pltpu.VMEM((n, 12 * C), BF16)] + big, 56, conv_flops, "last",
    )(flags, outer, inner, outer2, inner2, halo_o2, halo_i2, fold2, spread2, mask, conv_first, conv_second)
    return (updated.transpose(2, 0, 1), grad.transpose(2, 0, 1), g[0], g[1])


def solution(mesh):
    placed = (
        P(None, ("rep", "lat"), None),
        P(None, ("rep", "lat"), None),
        P("lat", None),
        P(),
        P(),
        P(),
    )
    return jax.shard_map(
        on_device,
        mesh=mesh,
        in_specs=placed,
        out_specs=(
            P(None, ("rep", "lat"), None),
            P(None, ("rep", "lat"), None),
            P(("rep", "lat"), None),
            P(("rep", "lat"), None),
        ),
        check_vma=False,
    )
```

```python
import functools

import jax
import jax.numpy as jnp
import numpy as np
from jax import lax
from jax.experimental import pallas as pl
from jax.experimental.pallas import tpu as pltpu
from jax.sharding import PartitionSpec as P

C = 128
F32 = jnp.float32
BF16 = jnp.bfloat16
SMEM = pl.BlockSpec(memory_space=pltpu.SMEM)
HBM = pl.BlockSpec(memory_space=pltpu.HBM)
MiB = 1 << 20
OUT, INN = 0, 1
FAR = 2
ROW = 3 * C
CONTRACT_LAST = (((1,), (1,)), ((), ()))
CONTRACT_ROWS = (((0,), (0,)), ((), ()))
FORWARD = ((OUT, OUT, 1), (OUT, INN, 2), (INN, OUT, 0), (INN, INN, 1), (INN, FAR, 2))
ADJOINT = ((OUT, OUT, 1), (INN, OUT, 2), (OUT, INN, 0), (INN, INN, 1), (INN, FAR, 0))
SCALE = np.float32(np.sqrt(2 / np.pi))
CUBE = np.float32(0.044715)
HALF = np.float32(0.5)
LINKS = {}


def chunk_of(n):
    for size in (432, 400, 384, 320, 256, 240, 144, 128, 80, 64, 48, 32, 16):
        if n % size == 0:
            return size
    return n


def put_taps(dst, at, row, adjoint):
    n = row.shape[0]
    wide = row.astype(F32)
    before = pltpu.roll(wide, 1, 0).astype(BF16)
    after = pltpu.roll(wide, n - 1, 0).astype(BF16)
    taps = (after, row, before) if adjoint else (before, row, after)
    for b, tap in enumerate(taps):
        dst[:, at + C * b : at + C * b + C] = tap


def row_tap(a, parity):
    return a + parity * (2 - 2 * a)


def build_forward(dst, w, parity):
    dst[...] = jnp.zeros_like(dst)
    for ro, ri, a in FORWARD:
        for b in range(3):
            at = ROW * ri + C * b
            dst[ro * C : ro * C + C, at : at + C] = w[3 * row_tap(a, parity) + b]


def build_adjoint(dst, w, parity):
    dst[...] = jnp.zeros_like(dst)
    for ro, ri, a in ADJOINT:
        for b in range(3):
            at = ROW * ri + C * b
            dst[at : at + C, ro * C : ro * C + C] = w[3 * row_tap(a, parity) + b]


def gelu_and_slope(x):
    square = x * x
    t = jnp.tanh(SCALE * (x + CUBE * (x * square)))
    cdf = HALF * (1.0 + t)
    slope = cdf + (HALF * x) * (1.0 - t * t) * (SCALE * (1.0 + np.float32(3) * CUBE * square))
    return x * cdf, slope


def over_chunks(n, step):
    m = chunk_of(n)

    def body(k, carry):
        step(pl.ds(pl.multiple_of(k * m, m), m))
        return carry

    lax.fori_loop(0, n // m, body, 0)


def near_forward(parity, rows, w, taps, fw, y):
    build_forward(fw, w, parity)
    for k in range(3):
        put_taps(taps, ROW * k, rows[k], False)
    y[...] = lax.dot_general(taps[...], fw[...], CONTRACT_LAST, preferred_element_type=F32)


def near_adjoint(parity, rows, w, taps, ad, d):
    build_adjoint(ad, w, parity)
    for k in range(3):
        put_taps(taps, ROW * k, rows[k], True)
    d[...] = jnp.dot(taps[...], ad[...], preferred_element_type=F32)


class Fetched:
    def __init__(self, src, dst, sem):
        self.ref, self.copy, self.done = dst, pltpu.make_async_copy(src, dst, sem), False
        self.copy.start()

    def now(self):
        if not self.done:
            self.copy.wait()
            self.done = True
        return self.ref


def start_kernel(flags, state, cotangent, mask, outs, wide, lines, cot, sems):
    parity = flags[0]
    outer, inner, mask_o, mask_i = outs
    n = outer.shape[1]
    lines = Fetched(mask, lines, sems.at[0])
    cots = [Fetched(cotangent.at[r], cot.at[k], sems.at[1 + k]) for k, r in ((0, parity), (1, 1 - parity))]
    states = [Fetched(state.at[r], p.at[0], sems.at[3 + k]) for k, r, p in ((0, parity, outer), (1, 1 - parity, inner))]
    wide[...] = jnp.zeros_like(wide)
    wide[0:2, 0:n] = lines.now()[...].astype(F32)
    for slot, pair, masks in ((0, outer, mask_o), (1, inner, mask_i)):
        cot = cots[slot].now()
        row = parity if slot == 0 else 1 - parity
        is_first = jnp.full((1, C), row, jnp.int32) == 0
        for at in range(0, n, C):
            size = min(C, n - at)
            line = jnp.where(is_first, wide[0:1, at : at + C], wide[1:2, at : at + C])
            tile = jnp.broadcast_to(line, (C, C)).T[:size]
            masks[at : at + size, :] = tile.astype(BF16)
            pair[1, at : at + size, :] = (cot[at : at + size, :].astype(F32) * tile).astype(BF16)
        states[slot].now()
        outs.send(slot)
        outs.send(2 + slot)


def first_kernel(
    flags, partner, outer, inner, halo, mask_i, w1, w2, outs, pre_o, dact_o, fold, spread,
    taps, utaps, fw, ad, y, d, src, dst, wide, wide_dst, row, sems
):
    parity = flags[0]
    n = src.shape[0]
    (inner2,) = outs
    outer, inner, w1, w2 = outer.now(), inner.now(), w1.now(), w2.now()
    halo = halo.now()
    near_forward(parity, (outer[0], inner[0], halo[0]), w1, taps, fw, y)
    pre = Fetched(y.at[:, pl.ds(0, C)], pre_o, sems.at[0])
    near_adjoint(parity, (outer[1], inner[1], halo[1]), w2, utaps, ad, d)
    dact = Fetched(d.at[:, pl.ds(0, C)], dact_o, sems.at[1])
    mask_i = mask_i.now()

    def finish(rows):
        keep = mask_i[rows, :].astype(F32)
        value, slope = gelu_and_slope(y[rows, C:])
        inner2[0, rows, :] = (keep * value).astype(BF16)
        inner2[1, rows, :] = (slope * (keep * d[rows, C:])).astype(BF16)

    over_chunks(n, finish)
    outs.send(0)

    @pl.when(flags[1] != 0)
    def _():
        src[...] = outer[0].astype(F32)
        u = outer[1].astype(F32)
        wide[:, 0:C] = pltpu.roll(u, n - 1, 0)
        wide[:, C : 2 * C] = u
        wide[:, 2 * C :] = pltpu.roll(u, 1, 0)

        def step(i, carry):
            for k in range(8):
                j = i * 8 + k
                at = partner[j]
                dst[pl.ds(j, 1), :] = src[pl.ds(at, 1), :]
                wide_dst[pl.ds(at, 1), :] = wide[pl.ds(j, 1), :]
            return carry

        lax.fori_loop(0, n // 8, step, 0)
        row[...] = dst[...].astype(BF16)
        pltpu.sync_copy(row, fold)
        for b in range(3):
            utaps[:, C * b : C * b + C] = wide_dst[:, C * b : C * b + C].astype(BF16)
        pltpu.sync_copy(utaps.at[:, pl.ds(0, ROW)], spread)

    pre.now()
    dact.now()


def top_copies(top, fold, row, spread, utaps, sems):
    copies = (pltpu.make_async_copy(fold, row, sems.at[0]), pltpu.make_async_copy(spread, utaps, sems.at[1]))

    @pl.when(top != 0)
    def _():
        for copy in copies:
            copy.start()

    return copies


def forward_taps(taps, halo, row, copy, top):
    @pl.when(top == 0)
    def _():
        put_taps(taps, 0, halo[...], False)

    @pl.when(top != 0)
    def _():
        copy.wait()
        put_taps(taps, 0, row[...], False)


def adjoint_taps(utaps, halo, copy, top):
    @pl.when(top == 0)
    def _():
        put_taps(utaps, 0, halo[...], True)

    @pl.when(top != 0)
    def _():
        copy.wait()


def far_kernel(
    flags, halo_s, w1, pre_o, mask_o, halo_g, w2, dact_o, fold, spread, outs, taps, utaps, y, d, row, sems
):
    parity, top = flags[0], flags[1]
    act, dpre = outs[0].at[0], outs[0].at[1]
    copies = top_copies(top, fold, row, spread, utaps, sems)
    halo_s, w1 = halo_s.now(), w1.now()
    forward_taps(taps, halo_s, row, copies[0], top)
    kernel = jnp.concatenate([w1[3 * row_tap(0, parity) + b] for b in range(3)], axis=1)
    y[...] = lax.dot_general(taps[...], kernel, CONTRACT_LAST, preferred_element_type=F32)
    halo_g, w2 = halo_g.now(), w2.now()
    adjoint_taps(utaps, halo_g, copies[1], top)
    a = row_tap(2 - 2 * top, parity)
    kernel = jnp.concatenate([w2[3 * a + b] for b in range(3)], axis=0)
    d[...] = jnp.dot(utaps[...], kernel, preferred_element_type=F32)
    pre_o, dact_o, mask_o = pre_o.now(), dact_o.now(), mask_o.now()

    def step(rows):
        keep = mask_o[rows, :].astype(F32)
        value, slope = gelu_and_slope(pre_o[rows, :] + y[rows, :])
        act[rows, :] = (keep * value).astype(BF16)
        dpre[rows, :] = (slope * (keep * (dact_o[rows, :] + d[rows, :]))).astype(BF16)

    over_chunks(y.shape[0], step)


def weights_kernel(
    flags, outer, inner, halo_in, halo_s, halo_g, outer2, inner2, fold, spread, spread2, outs,
    blank1, blank2, blank3, blank4, blank5, blank6, blank7, g1, g2, taps, utaps, htaps, hutaps, row, sems
):
    parity, top = flags[0], flags[1]
    keep, give = outs
    copies = top_copies(top, fold, row, spread, hutaps, sems)
    for k, pair in enumerate((outer, inner, halo_in)):
        pair = pair.now()
        put_taps(taps, ROW * k, pair[0], False)
        put_taps(utaps, ROW * k, pair[1], True)
    forward_taps(htaps, halo_s.now(), row, copies[0], top)
    adjoint_taps(hutaps, halo_g.now(), copies[1], top)
    outer2, inner2 = outer2.now(), inner2.now()
    act = jnp.concatenate([outer2[0], inner2[0]], axis=1)
    dpre = jnp.concatenate([outer2[1], inner2[1]], axis=1)
    p = lax.dot_general(dpre, taps[...], CONTRACT_ROWS, preferred_element_type=F32)
    q = lax.dot_general(outer2[1], htaps[...], CONTRACT_ROWS, preferred_element_type=F32)
    first, last = row_tap(0, parity), row_tap(2, parity)

    def block(x, r, k, b):
        return x[r * C : r * C + C, ROW * k + C * b : ROW * k + C * b + C]

    for b in range(3):
        g1[3 * first + b] = block(p, INN, OUT, b) + block(q, 0, 0, b)
        g1[3 + b] = block(p, OUT, OUT, b) + block(p, INN, INN, b)
        g1[3 * last + b] = block(p, OUT, INN, b) + block(p, INN, FAR, b)
    p = lax.dot_general(act, utaps[...], CONTRACT_ROWS, preferred_element_type=F32)
    q = lax.dot_general(outer2[0], hutaps[...], CONTRACT_ROWS, preferred_element_type=F32)
    is_top = jnp.full((C, C), top, jnp.int32) != 0
    for b in range(3):
        edge = block(q, 0, 0, b)
        g2[3 * first + b] = (block(p, OUT, INN, b) + block(p, INN, FAR, b) + jnp.where(is_top, edge, 0.0)).T
        g2[3 + b] = (block(p, OUT, OUT, b) + block(p, INN, INN, b)).T
        g2[3 * last + b] = (block(p, INN, OUT, b) + jnp.where(is_top, 0.0, edge)).T
    pairs, _, per, _ = keep.shape
    for here in range(2):

        @pl.when(parity == here)
        def _():
            for which, g in enumerate((g1, g2)):
                for owner in range(2 * pairs):
                    dst = keep if owner % 2 == here else give
                    at = owner * per
                    while at < (owner + 1) * per:
                        t = at // C
                        stop = min((owner + 1) * per, (t + 1) * C)
                        rows = slice(at - owner * per, stop - owner * per)
                        dst[owner // 2, which, rows, :] = g[t, at - t * C : stop - t * C, :]
                        at = stop


def second_forward_kernel(flags, outer2, inner2, halo, w2, outer, inner, mask_i, outs, taps, fw, y):
    upd_i, upd_o = outs
    outer2, inner2, halo, w2 = outer2.now(), inner2.now(), halo.now(), w2.now()
    near_forward(flags[0], (outer2[...], inner2[...], halo[...]), w2, taps, fw, y)
    outer, inner, mask_i = outer.now(), inner.now(), mask_i.now()

    def finish(rows):
        upd_o[rows, :] = outer[rows, :].astype(F32) + y[rows, :C]
        keep = mask_i[rows, :].astype(F32)
        upd_i[rows, :] = (keep * (inner[rows, :].astype(F32) + y[rows, C:])).astype(BF16)

    over_chunks(y.shape[0], finish)


def second_adjoint_kernel(flags, outer2, inner2, halo, w1, outer, inner, outs, taps, ad, d):
    grad_i, grad_o = outs
    outer2, inner2, halo, w1 = outer2.now(), inner2.now(), halo.now(), w1.now()
    near_adjoint(flags[0], (outer2[...], inner2[...], halo[...]), w1, taps, ad, d)
    outer, inner = outer.now(), inner.now()

    def finish(rows):
        grad_o[rows, :] = outer[rows, :].astype(F32) + d[rows, :C]
        grad_i[rows, :] = (inner[rows, :].astype(F32) + d[rows, C:]).astype(BF16)

    over_chunks(d.shape[0], finish)


def fold_act_kernel(flags, partner, outer2, fold, row, src, dst):
    @pl.when(flags[1] != 0)
    def _():
        pltpu.sync_copy(outer2.at[0], row)
        src[...] = row[...].astype(F32)

        def step(i, carry):
            for k in range(16):
                j = i * 16 + k
                dst[pl.ds(j, 1), :] = src[pl.ds(partner[j], 1), :]
            return carry

        lax.fori_loop(0, src.shape[0] // 16, step, 0)
        row[...] = dst[...].astype(BF16)
        pltpu.sync_copy(row, fold)


def fold_dpre_kernel(flags, partner, outer2, w1, spread, row, kernels, tap, term, total):
    @pl.when(flags[1] != 0)
    def _():
        pltpu.sync_copy(outer2.at[1], row)
        pltpu.sync_copy(w1, kernels)
        put_taps(tap, 0, row[...], True)
        kernel = jnp.concatenate([kernels[6 + b] for b in range(3)], axis=0)
        term[...] = jnp.dot(tap[...], kernel, preferred_element_type=F32)

        def step(i, carry):
            for k in range(16):
                j = i * 16 + k
                total[pl.ds(partner[j], 1), :] = term[pl.ds(j, 1), :]
            return carry

        lax.fori_loop(0, term.shape[0] // 16, step, 0)
        pltpu.sync_copy(total, spread)


def last_kernel(
    flags, halo, w2, w1, upd_o, mask_o, grad_o, upd_i, grad_i, fold, spread, updated, grad,
    taps, utaps, y, d, row, top_sems, out_u, out_g, sems
):
    parity, top = flags[0], flags[1]
    halo, w2 = halo.now(), w2.now()
    sent = []

    def send(src, dst):
        copy = pltpu.make_async_copy(src, dst, sems.at[len(sent)])
        copy.start()
        sent.append(copy)

    copies = top_copies(top, fold, row, spread, d, top_sems)
    forward_taps(taps, halo.at[0], row, copies[0], top)
    kernel = jnp.concatenate([w2[3 * row_tap(0, parity) + b] for b in range(3)], axis=1)
    y[...] = lax.dot_general(taps[...], kernel, CONTRACT_LAST, preferred_element_type=F32)
    w1, upd_o, mask_o = w1.now(), upd_o.now(), mask_o.now()

    def step(rows):
        out_u[rows, :] = (mask_o[rows, :].astype(F32) * (upd_o[rows, :] + y[rows, :])).astype(BF16)

    over_chunks(y.shape[0], step)
    send(out_u, updated.at[parity])
    send(upd_i.now(), updated.at[1 - parity])
    send(grad_i.now(), grad.at[1 - parity])

    @pl.when(top == 0)
    def _():
        put_taps(utaps, 0, halo[1], True)
        kernel = jnp.concatenate([w1[3 * row_tap(2, parity) + b] for b in range(3)], axis=0)
        d[...] = jnp.dot(utaps[...], kernel, preferred_element_type=F32)

    @pl.when(top != 0)
    def _():
        copies[1].wait()

    grad_o = grad_o.now()

    def step(rows):
        out_g[rows, :] = (grad_o[rows, :] + d[rows, :]).astype(BF16)

    over_chunks(y.shape[0], step)
    send(out_g, grad.at[parity])
    for copy in sent:
        copy.wait()


class Sent(tuple):
    def send(self, k):
        if k not in self.started:
            self.copies[k].start()
            self.started.append(k)


def call(kernel, scalars, operands, outs, scratch, limit, name, loose=(), loose_outs=()):
    n_in, n_out = len(operands), len(outs)
    shapes = [x[0].shape[1:] if isinstance(x, tuple) else x.shape for x in operands]
    arrays = [x[0] if isinstance(x, tuple) else x for x in operands]

    def run(*refs):
        refs = list(refs)

        def take(k):
            head = refs[:k]
            del refs[:k]
            return head

        small, given, free, results, free_out = (
            take(k) for k in (len(scalars), n_in, len(loose), n_out, len(loose_outs))
        )
        inside, made, sem_in, sem_out = take(n_in), take(n_out), *take(2)
        given = [g.at[x[1]] if isinstance(x, tuple) else g for g, x in zip(given, operands)]
        fetched = [Fetched(g, v, sem_in.at[k]) for k, (g, v) in enumerate(zip(given, inside))]
        sent = Sent(made)
        sent.started = []
        sent.copies = [pltpu.make_async_copy(v, r, sem_out.at[k]) for k, (v, r) in enumerate(zip(made, results))]
        kernel(*small, *fetched, *free, *([sent] if n_out else []), *free_out, *refs)
        for x in fetched:
            x.now()
        for k in range(n_out):
            sent.send(k)
        for copy in sent.copies:
            copy.wait()

    results = pl.pallas_call(
        run,
        in_specs=[SMEM] * len(scalars) + [HBM] * (n_in + len(loose)),
        out_specs=tuple(HBM for _ in range(n_out + len(loose_outs))),
        out_shape=tuple(outs) + tuple(loose_outs),
        scratch_shapes=[pltpu.VMEM(shape, x.dtype) for shape, x in zip(shapes, arrays)]
        + [pltpu.VMEM(x.shape, x.dtype) for x in outs]
        + [pltpu.SemaphoreType.DMA((max(1, n_in),)), pltpu.SemaphoreType.DMA((max(1, n_out),))]
        + list(scratch),
        compiler_params=pltpu.CompilerParams(vmem_limit_bytes=limit * MiB),
        cost_estimate=pl.CostEstimate(flops=1000, transcendentals=0, bytes_accessed=1000),
        name=name,
    )(*scalars, *arrays, *loose)
    return list(results)


def swap(x, n, inner):
    if inner:
        pairs = [(i, i ^ 1) for i in range(n)]
    else:
        pairs = [(i, i + 1) for i in range(1, n - 1, 2)]
        pairs = pairs + [(j, i) for i, j in pairs]
    return lax.ppermute(x, "lat", pairs)


def on_device(ocean_state, cotangent, land_mask, fold_partner, conv_first, conv_second):
    lat = lax.axis_size("lat")
    index = lax.axis_index("lat")
    n = ocean_state.shape[2]
    assert ocean_state.shape[1] == 2 and lat % 2 == 0
    bits = lat.bit_length() - 1
    parity = index & 1
    top = (index == lat - 1).astype(jnp.int32)
    order = list(range(2, bits)) + ([1] if bits > 1 else [])
    flags = jnp.stack([parity, top] + [(index >> bit) & 1 for bit in order]).astype(jnp.int32)
    row = jax.ShapeDtypeStruct((n, C), BF16)
    wide = jax.ShapeDtypeStruct((n, C), F32)
    pair = jax.ShapeDtypeStruct((2, n, C), BF16)
    taps1 = jax.ShapeDtypeStruct((n, ROW), BF16)
    per = 9 * C // lat
    part = jax.ShapeDtypeStruct((lat // 2, 2, per, C), F32)
    own = jax.ShapeDtypeStruct((per, C), F32)
    row_s, wide_s = pltpu.VMEM((n, C), BF16), pltpu.VMEM((n, C), F32)
    near_s = [pltpu.VMEM((n, 3 * ROW), BF16)] * 2 + [pltpu.VMEM((2 * C, 3 * ROW), BF16), pltpu.VMEM((3 * ROW, 2 * C), BF16)]
    near_s = near_s + [pltpu.VMEM((n, 2 * C), F32)] * 2
    dma = pltpu.SemaphoreType.DMA
    far_s = [pltpu.VMEM((n, ROW), BF16)] * 2 + [wide_s] * 2 + [row_s, dma((2,))]
    padded = pl.cdiv(n, C) * C

    outer, inner, mask_o, mask_i = call(
        start_kernel, (flags,), (), [pair, pair, row, row],
        [pltpu.VMEM((8, padded), F32), pltpu.VMEM((2, n), jnp.int32), pltpu.VMEM((2, n, C), BF16), dma((5,))],
        60, "start", loose=(ocean_state.transpose(1, 2, 0), cotangent.transpose(1, 2, 0), land_mask),
    )
    halo = swap(outer, lat, False)
    halo_in = swap(inner, lat, True)
    inner2, pre_o, dact_o, fold1, spread1 = call(
        first_kernel, (flags, fold_partner), (outer, inner, halo_in, mask_i, conv_first, conv_second), [pair],
        near_s + [wide_s, wide_s, pltpu.VMEM((n, ROW), F32), pltpu.VMEM((n, ROW), F32), row_s, dma((2,))], 60, "first",
        loose_outs=[wide, wide, row, taps1],
    )
    outer2 = call(
        far_kernel, (flags,), ((halo, 0), conv_first, pre_o, mask_o, (halo, 1), conv_second, dact_o), [pair],
        far_s, 60, "far", loose=(fold1, spread1),
    )[0]
    halo2 = swap(outer2, lat, False)
    halo_in2 = swap(inner2, lat, True)
    spread2, = call(
        fold_dpre_kernel, (flags, fold_partner), (), [],
        [row_s, pltpu.VMEM((9, C, C), BF16), pltpu.VMEM((n, ROW), BF16), wide_s, wide_s], 60, "fold_dpre",
        loose=(outer2, conv_first), loose_outs=[wide],
    )
    keep, give, own1, own2, *blank = call(
        weights_kernel, (flags,), (outer, inner, halo_in, (halo, 0), (halo, 1), outer2, inner2), [part, part],
        [pltpu.VMEM((9, C, C), F32)] * 2 + [pltpu.VMEM((n, 3 * ROW), BF16)] * 2
        + [pltpu.VMEM((n, ROW), BF16)] * 2 + [row_s, dma((2,))], 60, "wgrad", loose=(fold1, spread1, spread2),
        loose_outs=[own, own, row, wide, row, wide, row],
    )

    def body(carry):
        turn, given, _ = carry
        now = flags + 2 * turn
        arrived = swap(given, lat, True)
        g = (keep + arrived).reshape((2,) * (bits - 1) + (2, per, C))
        left = list(range(bits - 1, 0, -1))
        beside = []
        for stage, bit in enumerate(order):
            axis = left.index(bit)
            left.pop(axis)
            mine = ((index >> bit) + 2 * turn) & 1
            kept = lax.dynamic_index_in_dim(g, mine, axis, keepdims=False)
            go = lax.dynamic_index_in_dim(g, 1 - mine, axis, keepdims=False)
            if 1 <= stage <= 2:
                go, beside[stage - 1] = lax.optimization_barrier((go, beside[stage - 1]))
            pairs = [(i, i ^ (1 << bit)) for i in range(lat)]
            g = kept + lax.ppermute(go.astype(LINKS.get(stage, F32)), "lat", pairs).astype(F32)
            if stage == 0:
                beside.append(
                    call(
                        second_forward_kernel, (now,),
                        ((outer2, 0), (inner2, 0), (halo_in2, 0), conv_second, (outer, 0), (inner, 0), mask_i), [row, wide],
                        near_s[0:1] + near_s[2:3] + near_s[4:5], 28, "second",
                    )
                    + call(
                        fold_act_kernel, (now, fold_partner), (), [], [row_s, wide_s, wide_s], 16, "fold_act",
                        loose=(outer2,), loose_outs=[row],
                    )
                )
                beside.append(
                    call(
                        second_adjoint_kernel, (now,),
                        ((outer2, 1), (inner2, 1), (halo_in2, 1), conv_first, (outer, 1), (inner, 1)), [row, wide],
                        near_s[0:1] + near_s[3:4] + near_s[4:5], 28, "second_adjoint",
                    )
                )
        return turn + 1, arrived, ([g[0], g[1]], beside)

    stop = jnp.minimum(1, parity + 1)
    start = ([own1, own2], [[blank[0], blank[1], blank[4]], [blank[2], blank[3]]])
    _, _, ((g1, g2), (near, near_a)) = lax.while_loop(lambda c: c[0] < stop, body, (jnp.int32(0), give, start))
    fold2 = near[2], spread2
    (upd_i, upd_o), (grad_i, grad_o) = near[:2], near_a[:2]
    updated, grad = call(
        last_kernel, (flags,), (halo2, conv_second, conv_first, upd_o, mask_o, grad_o, upd_i, grad_i), [],
        far_s + [row_s, row_s, dma((4,))], 28, "last", loose=tuple(fold2), loose_outs=[pair, pair],
    )
    return (updated.transpose(2, 0, 1), grad.transpose(2, 0, 1), g1, g2)


def solution(mesh):
    placed = (
        P(None, ("rep", "lat"), None),
        P(None, ("rep", "lat"), None),
        P("lat", None),
        P(),
        P(),
        P(),
    )
    return jax.shard_map(
        on_device,
        mesh=mesh,
        in_specs=placed,
        out_specs=(
            P(None, ("rep", "lat"), None),
            P(None, ("rep", "lat"), None),
            P(("rep", "lat"), None),
            P(("rep", "lat"), None),
        ),
        check_vma=False,
    )
```

```python
import functools

import jax
import jax.numpy as jnp
import numpy as np
from jax import lax
from jax.experimental import pallas as pl
from jax.experimental.pallas import tpu as pltpu
from jax.sharding import PartitionSpec as P

C = 128
F32 = jnp.float32
BF16 = jnp.bfloat16
SMEM = pl.BlockSpec(memory_space=pltpu.SMEM)
VMEM = pl.BlockSpec(memory_space=pltpu.VMEM)
HBM = pl.BlockSpec(memory_space=pltpu.HBM)
MiB = 1 << 20
OUT, INN = 0, 1
FAR = 2
ROW = 3 * C
CONTRACT_LAST = (((1,), (1,)), ((), ()))
CONTRACT_ROWS = (((0,), (0,)), ((), ()))
FORWARD = ((OUT, OUT, 1), (OUT, INN, 2), (INN, OUT, 0), (INN, INN, 1), (INN, FAR, 2))
ADJOINT = ((OUT, OUT, 1), (INN, OUT, 2), (OUT, INN, 0), (INN, INN, 1), (INN, FAR, 0))
SCALE = np.float32(np.sqrt(2 / np.pi))
CUBE = np.float32(0.044715)
HALF = np.float32(0.5)


def chunk_of(n):
    for size in (432, 400, 384, 320, 256, 240, 144, 128, 80, 64, 48, 32, 16):
        if n % size == 0:
            return size
    return n


def put_taps(dst, at, row, adjoint):
    n = row.shape[0]
    wide = row.astype(F32)
    before = pltpu.roll(wide, 1, 0).astype(BF16)
    after = pltpu.roll(wide, n - 1, 0).astype(BF16)
    taps = (after, row, before) if adjoint else (before, row, after)
    for b, tap in enumerate(taps):
        dst[:, at + C * b : at + C * b + C] = tap


def row_tap(a, parity):
    return a + parity * (2 - 2 * a)


def build_forward(dst, w, parity):
    dst[...] = jnp.zeros_like(dst)
    for ro, ri, a in FORWARD:
        for b in range(3):
            at = ROW * ri + C * b
            dst[ro * C : ro * C + C, at : at + C] = w[3 * row_tap(a, parity) + b]


def build_adjoint(dst, w, parity):
    dst[...] = jnp.zeros_like(dst)
    for ro, ri, a in ADJOINT:
        for b in range(3):
            at = ROW * ri + C * b
            dst[at : at + C, ro * C : ro * C + C] = w[3 * row_tap(a, parity) + b]


def gelu_and_slope(x):
    square = x * x
    t = jnp.tanh(SCALE * (x + CUBE * (x * square)))
    cdf = HALF * (1.0 + t)
    slope = cdf + (HALF * x) * (1.0 - t * t) * (SCALE * (1.0 + np.float32(3) * CUBE * square))
    return x * cdf, slope


def over_chunks(n, step):
    m = chunk_of(n)

    def body(k, carry):
        step(pl.ds(pl.multiple_of(k * m, m), m))
        return carry

    lax.fori_loop(0, n // m, body, 0)


def near_forward(parity, rows, w, taps, fw, y):
    build_forward(fw, w, parity)
    for k in range(3):
        put_taps(taps, ROW * k, rows[k], False)
    y[...] = lax.dot_general(taps[...], fw[...], CONTRACT_LAST, preferred_element_type=F32)


def near_adjoint(parity, rows, w, taps, ad, d):
    build_adjoint(ad, w, parity)
    for k in range(3):
        put_taps(taps, ROW * k, rows[k], True)
    d[...] = jnp.dot(taps[...], ad[...], preferred_element_type=F32)


class Fetched:
    def __init__(self, src, dst, sem):
        self.ref, self.copy, self.done = dst, pltpu.make_async_copy(src, dst, sem), False
        self.copy.start()

    def now(self):
        if not self.done:
            self.copy.wait()
            self.done = True
        return self.ref


def start_kernel(flags, state, cotangent, mask, outs, wide, lines, cot, sems):
    parity = flags[0]
    outer, inner, mask_o, mask_i = outs
    n = outer.shape[1]
    lines = Fetched(mask, lines, sems.at[0])
    cots = [Fetched(cotangent.at[r], cot.at[k], sems.at[1 + k]) for k, r in ((0, parity), (1, 1 - parity))]
    states = [Fetched(state.at[r], p.at[0], sems.at[3 + k]) for k, r, p in ((0, parity, outer), (1, 1 - parity, inner))]
    wide[...] = jnp.zeros_like(wide)
    wide[0:2, 0:n] = lines.now()[...].astype(F32)
    for slot, pair, masks in ((0, outer, mask_o), (1, inner, mask_i)):
        cot = cots[slot].now()
        row = parity if slot == 0 else 1 - parity
        is_first = jnp.full((1, C), row, jnp.int32) == 0
        for at in range(0, n, C):
            size = min(C, n - at)
            line = jnp.where(is_first, wide[0:1, at : at + C], wide[1:2, at : at + C])
            tile = jnp.broadcast_to(line, (C, C)).T[:size]
            masks[at : at + size, :] = tile.astype(BF16)
            pair[1, at : at + size, :] = (cot[at : at + size, :].astype(F32) * tile).astype(BF16)
        states[slot].now()
        outs.send(slot)
        outs.send(2 + slot)


def first_kernel(
    flags, partner, outer, inner, halo, mask_i, w1, w2, outs, pre_o, dact_o, fold, spread,
    taps, utaps, fw, ad, y, d, src, dst, wide, wide_dst, row, sems
):
    parity = flags[0]
    n = src.shape[0]
    (inner2,) = outs
    outer, inner, w1, w2 = outer.now(), inner.now(), w1.now(), w2.now()
    halo = halo.now()
    near_forward(parity, (outer[0], inner[0], halo[0]), w1, taps, fw, y)
    pre = Fetched(y.at[:, pl.ds(0, C)], pre_o, sems.at[0])
    near_adjoint(parity, (outer[1], inner[1], halo[1]), w2, utaps, ad, d)
    dact = Fetched(d.at[:, pl.ds(0, C)], dact_o, sems.at[1])
    mask_i = mask_i.now()

    def finish(rows):
        keep = mask_i[rows, :].astype(F32)
        value, slope = gelu_and_slope(y[rows, C:])
        inner2[0, rows, :] = (keep * value).astype(BF16)
        inner2[1, rows, :] = (slope * (keep * d[rows, C:])).astype(BF16)

    over_chunks(n, finish)
    outs.send(0)

    @pl.when(flags[1] != 0)
    def _():
        src[...] = outer[0].astype(F32)
        u = outer[1].astype(F32)
        wide[:, 0:C] = pltpu.roll(u, n - 1, 0)
        wide[:, C : 2 * C] = u
        wide[:, 2 * C :] = pltpu.roll(u, 1, 0)

        def step(i, carry):
            for k in range(8):
                j = i * 8 + k
                at = partner[j]
                dst[pl.ds(j, 1), :] = src[pl.ds(at, 1), :]
                wide_dst[pl.ds(at, 1), :] = wide[pl.ds(j, 1), :]
            return carry

        lax.fori_loop(0, n // 8, step, 0)
        row[...] = dst[...].astype(BF16)
        pltpu.sync_copy(row, fold)
        for b in range(3):
            utaps[:, C * b : C * b + C] = wide_dst[:, C * b : C * b + C].astype(BF16)
        pltpu.sync_copy(utaps.at[:, pl.ds(0, ROW)], spread)

    pre.now()
    dact.now()


def top_copies(top, fold, row, spread, utaps, sems):
    copies = (pltpu.make_async_copy(fold, row, sems.at[0]), pltpu.make_async_copy(spread, utaps, sems.at[1]))

    @pl.when(top != 0)
    def _():
        for copy in copies:
            copy.start()

    return copies


def forward_taps(taps, halo, row, copy, top):
    @pl.when(top == 0)
    def _():
        put_taps(taps, 0, halo[...], False)

    @pl.when(top != 0)
    def _():
        copy.wait()
        put_taps(taps, 0, row[...], False)


def adjoint_taps(utaps, halo, copy, top):
    @pl.when(top == 0)
    def _():
        put_taps(utaps, 0, halo[...], True)

    @pl.when(top != 0)
    def _():
        copy.wait()


def far_kernel(
    flags, halo_s, w1, pre_o, mask_o, halo_g, w2, dact_o, fold, spread, outs, taps, utaps, y, d, row, sems
):
    parity, top = flags[0], flags[1]
    act, dpre = outs[0].at[0], outs[0].at[1]
    copies = top_copies(top, fold, row, spread, utaps, sems)
    halo_s, w1 = halo_s.now(), w1.now()
    forward_taps(taps, halo_s, row, copies[0], top)
    kernel = jnp.concatenate([w1[3 * row_tap(0, parity) + b] for b in range(3)], axis=1)
    y[...] = lax.dot_general(taps[...], kernel, CONTRACT_LAST, preferred_element_type=F32)
    halo_g, w2 = halo_g.now(), w2.now()
    adjoint_taps(utaps, halo_g, copies[1], top)
    a = row_tap(2 - 2 * top, parity)
    kernel = jnp.concatenate([w2[3 * a + b] for b in range(3)], axis=0)
    d[...] = jnp.dot(utaps[...], kernel, preferred_element_type=F32)
    pre_o, dact_o, mask_o = pre_o.now(), dact_o.now(), mask_o.now()

    def step(rows):
        keep = mask_o[rows, :].astype(F32)
        value, slope = gelu_and_slope(pre_o[rows, :] + y[rows, :])
        act[rows, :] = (keep * value).astype(BF16)
        dpre[rows, :] = (slope * (keep * (dact_o[rows, :] + d[rows, :]))).astype(BF16)

    over_chunks(y.shape[0], step)


def weights_kernel(
    flags, partner, outer, inner, halo_in, halo_s, halo_g, outer2, inner2, fold, spread, w1, outs,
    spread2, blank1, blank2, blank3, blank4, blank5, blank6, blank7,
    g1, g2, taps, utaps, htaps, hutaps, row, sems, term, total
):
    parity, top = flags[0], flags[1]
    keep, give = outs
    copies = top_copies(top, fold, row, spread, hutaps, sems)
    for k, pair in enumerate((outer, inner, halo_in)):
        pair = pair.now()
        put_taps(taps, ROW * k, pair[0], False)
        put_taps(utaps, ROW * k, pair[1], True)
    forward_taps(htaps, halo_s.now(), row, copies[0], top)
    adjoint_taps(hutaps, halo_g.now(), copies[1], top)
    outer2, inner2 = outer2.now(), inner2.now()
    act = jnp.concatenate([outer2[0], inner2[0]], axis=1)
    dpre = jnp.concatenate([outer2[1], inner2[1]], axis=1)
    p = lax.dot_general(dpre, taps[...], CONTRACT_ROWS, preferred_element_type=F32)
    q = lax.dot_general(outer2[1], htaps[...], CONTRACT_ROWS, preferred_element_type=F32)
    first, last = row_tap(0, parity), row_tap(2, parity)

    def block(x, r, k, b):
        return x[r * C : r * C + C, ROW * k + C * b : ROW * k + C * b + C]

    for b in range(3):
        g1[3 * first + b] = block(p, INN, OUT, b) + block(q, 0, 0, b)
        g1[3 + b] = block(p, OUT, OUT, b) + block(p, INN, INN, b)
        g1[3 * last + b] = block(p, OUT, INN, b) + block(p, INN, FAR, b)
    p = lax.dot_general(act, utaps[...], CONTRACT_ROWS, preferred_element_type=F32)
    q = lax.dot_general(outer2[0], hutaps[...], CONTRACT_ROWS, preferred_element_type=F32)
    is_top = jnp.full((C, C), top, jnp.int32) != 0
    for b in range(3):
        edge = block(q, 0, 0, b)
        g2[3 * first + b] = (block(p, OUT, INN, b) + block(p, INN, FAR, b) + jnp.where(is_top, edge, 0.0)).T
        g2[3 + b] = (block(p, OUT, OUT, b) + block(p, INN, INN, b)).T
        g2[3 * last + b] = (block(p, INN, OUT, b) + jnp.where(is_top, 0.0, edge)).T
    pairs, _, per, _ = keep.shape
    for here in range(2):

        @pl.when(parity == here)
        def _():
            for which, g in enumerate((g1, g2)):
                for owner in range(2 * pairs):
                    dst = keep if owner % 2 == here else give
                    at = owner * per
                    while at < (owner + 1) * per:
                        t = at // C
                        stop = min((owner + 1) * per, (t + 1) * C)
                        rows = slice(at - owner * per, stop - owner * per)
                        dst[owner // 2, which, rows, :] = g[t, at - t * C : stop - t * C, :]
                        at = stop
    outs.send(0)
    outs.send(1)

    @pl.when(top != 0)
    def _():
        put_taps(hutaps, 0, outer2[1], True)
        pltpu.sync_copy(w1.at[6], htaps.at[pl.ds(0, C), pl.ds(0, C)])
        pltpu.sync_copy(w1.at[7], htaps.at[pl.ds(C, C), pl.ds(0, C)])
        pltpu.sync_copy(w1.at[8], htaps.at[pl.ds(2 * C, C), pl.ds(0, C)])
        term[...] = jnp.dot(hutaps[...], htaps[: 3 * C, :C], preferred_element_type=F32)

        def step(i, carry):
            for k in range(16):
                j = i * 16 + k
                total[pl.ds(partner[j], 1), :] = term[pl.ds(j, 1), :]
            return carry

        lax.fori_loop(0, term.shape[0] // 16, step, 0)
        pltpu.sync_copy(total, spread2)


def second_forward_kernel(flags, outer2, inner2, halo, w2, outer, inner, mask_i, outs, taps, fw, y):
    upd_i, upd_o = outs
    outer2, inner2, halo, w2 = outer2.now(), inner2.now(), halo.now(), w2.now()
    near_forward(flags[0], (outer2[...], inner2[...], halo[...]), w2, taps, fw, y)
    outer, inner, mask_i = outer.now(), inner.now(), mask_i.now()

    def finish(rows):
        upd_o[rows, :] = outer[rows, :].astype(F32) + y[rows, :C]
        keep = mask_i[rows, :].astype(F32)
        upd_i[rows, :] = (keep * (inner[rows, :].astype(F32) + y[rows, C:])).astype(BF16)

    over_chunks(y.shape[0], finish)


def second_adjoint_kernel(flags, outer2, inner2, halo, w1, outer, inner, outs, taps, ad, d):
    grad_i, grad_o = outs
    outer2, inner2, halo, w1 = outer2.now(), inner2.now(), halo.now(), w1.now()
    near_adjoint(flags[0], (outer2[...], inner2[...], halo[...]), w1, taps, ad, d)
    outer, inner = outer.now(), inner.now()

    def finish(rows):
        grad_o[rows, :] = outer[rows, :].astype(F32) + d[rows, :C]
        grad_i[rows, :] = (inner[rows, :].astype(F32) + d[rows, C:]).astype(BF16)

    over_chunks(d.shape[0], finish)


def fold_act_kernel(flags, partner, outer2, fold, row, src, dst):
    @pl.when(flags[1] != 0)
    def _():
        pltpu.sync_copy(outer2.at[0], row)
        src[...] = row[...].astype(F32)

        def step(i, carry):
            for k in range(16):
                j = i * 16 + k
                dst[pl.ds(j, 1), :] = src[pl.ds(partner[j], 1), :]
            return carry

        lax.fori_loop(0, src.shape[0] // 16, step, 0)
        row[...] = dst[...].astype(BF16)
        pltpu.sync_copy(row, fold)


def halve_kernel(which, flags, kept, taken, go, stay):
    mine = flags[which]
    for at in range(kept.shape[0]):
        go[at] = kept[at, 1 - mine] + taken[at, 1 - mine]
        stay[at] = kept[at, mine] + taken[at, mine]


def total_kernel(kept, taken, first, second):
    first[...] = kept[0] + taken[0]
    second[...] = kept[1] + taken[1]


def last_kernel(
    flags, halo, w2, w1, upd_o, mask_o, grad_o, upd_i, grad_i, fold, spread, updated, grad,
    taps, utaps, y, d, row, top_sems, out_u, out_g, sems
):
    parity, top = flags[0], flags[1]
    halo, w2 = halo.now(), w2.now()
    sent = []

    def send(src, dst):
        copy = pltpu.make_async_copy(src, dst, sems.at[len(sent)])
        copy.start()
        sent.append(copy)

    copies = top_copies(top, fold, row, spread, d, top_sems)
    forward_taps(taps, halo.at[0], row, copies[0], top)
    kernel = jnp.concatenate([w2[3 * row_tap(0, parity) + b] for b in range(3)], axis=1)
    y[...] = lax.dot_general(taps[...], kernel, CONTRACT_LAST, preferred_element_type=F32)
    w1, upd_o, mask_o = w1.now(), upd_o.now(), mask_o.now()

    def step(rows):
        out_u[rows, :] = (mask_o[rows, :].astype(F32) * (upd_o[rows, :] + y[rows, :])).astype(BF16)

    over_chunks(y.shape[0], step)
    send(out_u, updated.at[parity])
    send(upd_i.now(), updated.at[1 - parity])
    send(grad_i.now(), grad.at[1 - parity])

    @pl.when(top == 0)
    def _():
        put_taps(utaps, 0, halo[1], True)
        kernel = jnp.concatenate([w1[3 * row_tap(2, parity) + b] for b in range(3)], axis=0)
        d[...] = jnp.dot(utaps[...], kernel, preferred_element_type=F32)

    @pl.when(top != 0)
    def _():
        copies[1].wait()

    grad_o = grad_o.now()

    def step(rows):
        out_g[rows, :] = (grad_o[rows, :] + d[rows, :]).astype(BF16)

    over_chunks(y.shape[0], step)
    send(out_g, grad.at[parity])
    for copy in sent:
        copy.wait()


class Sent(tuple):
    def send(self, k):
        if k not in self.started:
            self.copies[k].start()
            self.started.append(k)


def call(kernel, scalars, operands, outs, scratch, limit, name, loose=(), loose_outs=()):
    n_in, n_out = len(operands), len(outs)
    shapes = [x[0].shape[1:] if isinstance(x, tuple) else x.shape for x in operands]
    arrays = [x[0] if isinstance(x, tuple) else x for x in operands]

    def run(*refs):
        refs = list(refs)

        def take(k):
            head = refs[:k]
            del refs[:k]
            return head

        small, given, free, results, free_out = (
            take(k) for k in (len(scalars), n_in, len(loose), n_out, len(loose_outs))
        )
        inside, made, sem_in, sem_out = take(n_in), take(n_out), *take(2)
        given = [g.at[x[1]] if isinstance(x, tuple) else g for g, x in zip(given, operands)]
        fetched = [Fetched(g, v, sem_in.at[k]) for k, (g, v) in enumerate(zip(given, inside))]
        sent = Sent(made)
        sent.started = []
        sent.copies = [pltpu.make_async_copy(v, r, sem_out.at[k]) for k, (v, r) in enumerate(zip(made, results))]
        kernel(*small, *fetched, *free, *([sent] if n_out else []), *free_out, *refs)
        for x in fetched:
            x.now()
        for k in range(n_out):
            sent.send(k)
        for copy in sent.copies:
            copy.wait()

    results = pl.pallas_call(
        run,
        in_specs=[SMEM] * len(scalars) + [HBM] * (n_in + len(loose)),
        out_specs=tuple(HBM for _ in range(n_out + len(loose_outs))),
        out_shape=tuple(outs) + tuple(loose_outs),
        scratch_shapes=[pltpu.VMEM(shape, x.dtype) for shape, x in zip(shapes, arrays)]
        + [pltpu.VMEM(x.shape, x.dtype) for x in outs]
        + [pltpu.SemaphoreType.DMA((max(1, n_in),)), pltpu.SemaphoreType.DMA((max(1, n_out),))]
        + list(scratch),
        compiler_params=pltpu.CompilerParams(vmem_limit_bytes=limit * MiB),
        cost_estimate=pl.CostEstimate(flops=1000, transcendentals=0, bytes_accessed=1000),
        name=name,
    )(*scalars, *arrays, *loose)
    return list(results)


def swap(x, n, inner):
    if inner:
        pairs = [(i, i ^ 1) for i in range(n)]
    else:
        pairs = [(i, i + 1) for i in range(1, n - 1, 2)]
        pairs = pairs + [(j, i) for i, j in pairs]
    return lax.ppermute(x, "lat", pairs)


def on_device(ocean_state, cotangent, land_mask, fold_partner, conv_first, conv_second):
    lat = lax.axis_size("lat")
    index = lax.axis_index("lat")
    n = ocean_state.shape[2]
    assert ocean_state.shape[1] == 2 and lat % 2 == 0
    bits = lat.bit_length() - 1
    parity = index & 1
    top = (index == lat - 1).astype(jnp.int32)
    order = list(range(2, bits)) + ([1] if bits > 1 else [])
    flags = jnp.stack([parity, top] + [(index >> bit) & 1 for bit in order]).astype(jnp.int32)
    row = jax.ShapeDtypeStruct((n, C), BF16)
    wide = jax.ShapeDtypeStruct((n, C), F32)
    pair = jax.ShapeDtypeStruct((2, n, C), BF16)
    taps1 = jax.ShapeDtypeStruct((n, ROW), BF16)
    per = 9 * C // lat
    part = jax.ShapeDtypeStruct((lat // 2, 2, per, C), F32)
    own = jax.ShapeDtypeStruct((per, C), F32)
    row_s, wide_s = pltpu.VMEM((n, C), BF16), pltpu.VMEM((n, C), F32)
    near_s = [pltpu.VMEM((n, 3 * ROW), BF16)] * 2 + [pltpu.VMEM((2 * C, 3 * ROW), BF16), pltpu.VMEM((3 * ROW, 2 * C), BF16)]
    near_s = near_s + [pltpu.VMEM((n, 2 * C), F32)] * 2
    dma = pltpu.SemaphoreType.DMA
    far_s = [pltpu.VMEM((n, ROW), BF16)] * 2 + [wide_s] * 2 + [row_s, dma((2,))]
    padded = pl.cdiv(n, C) * C

    outer, inner, mask_o, mask_i = call(
        start_kernel, (flags,), (), [pair, pair, row, row],
        [pltpu.VMEM((8, padded), F32), pltpu.VMEM((2, n), jnp.int32), pltpu.VMEM((2, n, C), BF16), dma((5,))],
        60, "start", loose=(ocean_state.transpose(1, 2, 0), cotangent.transpose(1, 2, 0), land_mask),
    )
    halo = swap(outer, lat, False)
    halo_in = swap(inner, lat, True)
    inner2, pre_o, dact_o, fold1, spread1 = call(
        first_kernel, (flags, fold_partner), (outer, inner, halo_in, mask_i, conv_first, conv_second), [pair],
        near_s + [wide_s, wide_s, pltpu.VMEM((n, ROW), F32), pltpu.VMEM((n, ROW), F32), row_s, dma((2,))], 60, "first",
        loose_outs=[wide, wide, row, taps1],
    )
    outer2 = call(
        far_kernel, (flags,), ((halo, 0), conv_first, pre_o, mask_o, (halo, 1), conv_second, dact_o), [pair],
        far_s, 60, "far", loose=(fold1, spread1),
    )[0]
    halo2 = swap(outer2, lat, False)
    halo_in2 = swap(inner2, lat, True)
    keep, give, spread2, own1, own2, *blank = call(
        weights_kernel, (flags, fold_partner), (outer, inner, halo_in, (halo, 0), (halo, 1), outer2, inner2), [part, part],
        [pltpu.VMEM((9, C, C), F32)] * 2 + [pltpu.VMEM((n, 3 * ROW), BF16)] * 2
        + [pltpu.VMEM((n, ROW), BF16)] * 2 + [row_s, dma((2,)), wide_s, wide_s], 60, "wgrad",
        loose=(fold1, spread1, conv_first), loose_outs=[wide, own, own, row, wide, row, wide, row],
    )

    def body(carry):
        turn, given, _ = carry
        now = flags + 2 * turn
        arrived = swap(given, lat, True)
        kept, taken = keep, arrived
        params = pltpu.CompilerParams(vmem_limit_bytes=8 * MiB)
        cost = pl.CostEstimate(flops=1000, transcendentals=0, bytes_accessed=1000)
        left = list(range(bits - 1, 0, -1))
        beside = []
        for stage, bit in enumerate(order):
            axis = left.index(bit)
            split = (2**axis, 2, 2 ** (len(left) - axis - 1) * 2, per, C)
            left.pop(axis)
            half = jax.ShapeDtypeStruct(split[:1] + split[2:], F32)
            go, kept = pl.pallas_call(
                functools.partial(halve_kernel, 2 + stage), in_specs=[SMEM, VMEM, VMEM], out_specs=(VMEM, VMEM),
                out_shape=(half, half), compiler_params=params, cost_estimate=cost, name=f"halve{stage}",
            )(now, kept.reshape(split), taken.reshape(split))
            if 1 <= stage <= 2:
                go, beside[stage - 1] = lax.optimization_barrier((go, beside[stage - 1]))
            pairs = [(i, i ^ (1 << bit)) for i in range(lat)]
            taken = lax.ppermute(go, "lat", pairs)
            if stage == 0:
                beside.append(
                    call(
                        second_forward_kernel, (now,),
                        ((outer2, 0), (inner2, 0), (halo_in2, 0), conv_second, (outer, 0), (inner, 0), mask_i), [row, wide],
                        near_s[0:1] + near_s[2:3] + near_s[4:5], 28, "second",
                    )
                    + call(
                        fold_act_kernel, (now, fold_partner), (), [], [row_s, wide_s, wide_s], 16, "fold_act",
                        loose=(outer2,), loose_outs=[row],
                    )
                )
                beside.append(
                    call(
                        second_adjoint_kernel, (now,),
                        ((outer2, 1), (inner2, 1), (halo_in2, 1), conv_first, (outer, 1), (inner, 1)), [row, wide],
                        near_s[0:1] + near_s[3:4] + near_s[4:5], 28, "second_adjoint",
                    )
                )
        total = pl.pallas_call(
            total_kernel, in_specs=[VMEM, VMEM], out_specs=(VMEM, VMEM), out_shape=(own, own), compiler_params=params,
            cost_estimate=cost, name="total",
        )(kept.reshape(2, per, C), taken.reshape(2, per, C))
        return turn + 1, arrived, (list(total), beside)

    stop = jnp.minimum(1, parity + 1)
    start = ([own1, own2], [[blank[0], blank[1], blank[4]], [blank[2], blank[3]]])
    _, _, ((g1, g2), (near, near_a)) = lax.while_loop(lambda c: c[0] < stop, body, (jnp.int32(0), give, start))
    fold2 = near[2], spread2
    (upd_i, upd_o), (grad_i, grad_o) = near[:2], near_a[:2]
    updated, grad = call(
        last_kernel, (flags,), (halo2, conv_second, conv_first, upd_o, mask_o, grad_o, upd_i, grad_i), [],
        far_s + [row_s, row_s, dma((4,))], 28, "last", loose=tuple(fold2), loose_outs=[pair, pair],
    )
    return (updated.transpose(2, 0, 1), grad.transpose(2, 0, 1), g1, g2)


def solution(mesh):
    placed = (
        P(None, ("rep", "lat"), None),
        P(None, ("rep", "lat"), None),
        P("lat", None),
        P(),
        P(),
        P(),
    )
    return jax.shard_map(
        on_device,
        mesh=mesh,
        in_specs=placed,
        out_specs=(
            P(None, ("rep", "lat"), None),
            P(None, ("rep", "lat"), None),
            P(("rep", "lat"), None),
            P(("rep", "lat"), None),
        ),
        check_vma=False,
    )
```

```python
import functools

import jax
import jax.numpy as jnp
import numpy as np
from jax import lax
from jax.experimental import pallas as pl
from jax.experimental.pallas import tpu as pltpu
from jax.sharding import PartitionSpec as P

C = 128
F32 = jnp.float32
BF16 = jnp.bfloat16
SMEM = pl.BlockSpec(memory_space=pltpu.SMEM)
VMEM = pl.BlockSpec(memory_space=pltpu.VMEM)
HBM = pl.BlockSpec(memory_space=pltpu.HBM)
MiB = 1 << 20
OUT, INN = 0, 1
FAR = 2
ROW = 3 * C
CONTRACT_LAST = (((1,), (1,)), ((), ()))
CONTRACT_ROWS = (((0,), (0,)), ((), ()))
FORWARD = ((OUT, OUT, 1), (OUT, INN, 2), (INN, OUT, 0), (INN, INN, 1), (INN, FAR, 2))
ADJOINT = ((OUT, OUT, 1), (INN, OUT, 2), (OUT, INN, 0), (INN, INN, 1), (INN, FAR, 0))
SCALE = np.float32(np.sqrt(2 / np.pi))
CUBE = np.float32(0.044715)
HALF = np.float32(0.5)
LINKS = {0: BF16, 1: BF16}


def chunk_of(n):
    for size in (432, 400, 384, 320, 256, 240, 144, 128, 80, 64, 48, 32, 16):
        if n % size == 0:
            return size
    return n


def put_taps(dst, at, row, adjoint):
    n = row.shape[0]
    wide = row.astype(F32)
    before = pltpu.roll(wide, 1, 0).astype(BF16)
    after = pltpu.roll(wide, n - 1, 0).astype(BF16)
    taps = (after, row, before) if adjoint else (before, row, after)
    for b, tap in enumerate(taps):
        dst[:, at + C * b : at + C * b + C] = tap


def row_tap(a, parity):
    return a + parity * (2 - 2 * a)


def build_forward(dst, w, parity):
    dst[...] = jnp.zeros_like(dst)
    for ro, ri, a in FORWARD:
        for b in range(3):
            at = ROW * ri + C * b
            dst[ro * C : ro * C + C, at : at + C] = w[3 * row_tap(a, parity) + b]


def build_adjoint(dst, w, parity):
    dst[...] = jnp.zeros_like(dst)
    for ro, ri, a in ADJOINT:
        for b in range(3):
            at = ROW * ri + C * b
            dst[at : at + C, ro * C : ro * C + C] = w[3 * row_tap(a, parity) + b]


def gelu_and_slope(x):
    square = x * x
    t = jnp.tanh(SCALE * (x + CUBE * (x * square)))
    cdf = HALF * (1.0 + t)
    slope = cdf + (HALF * x) * (1.0 - t * t) * (SCALE * (1.0 + np.float32(3) * CUBE * square))
    return x * cdf, slope


def over_chunks(n, step):
    m = chunk_of(n)

    def body(k, carry):
        step(pl.ds(pl.multiple_of(k * m, m), m))
        return carry

    lax.fori_loop(0, n // m, body, 0)


def near_forward(parity, rows, w, taps, fw, y):
    build_forward(fw, w, parity)
    for k in range(3):
        put_taps(taps, ROW * k, rows[k], False)
    y[...] = lax.dot_general(taps[...], fw[...], CONTRACT_LAST, preferred_element_type=F32)


def near_adjoint(parity, rows, w, taps, ad, d):
    build_adjoint(ad, w, parity)
    for k in range(3):
        put_taps(taps, ROW * k, rows[k], True)
    d[...] = jnp.dot(taps[...], ad[...], preferred_element_type=F32)


class Fetched:
    def __init__(self, src, dst, sem):
        self.ref, self.copy, self.done = dst, pltpu.make_async_copy(src, dst, sem), False
        self.copy.start()

    def now(self):
        if not self.done:
            self.copy.wait()
            self.done = True
        return self.ref


def start_kernel(flags, state, cotangent, mask, outs, wide, lines, cot, sems):
    parity = flags[0]
    outer, inner, mask_o, mask_i = outs
    n = outer.shape[1]
    lines = Fetched(mask, lines, sems.at[0])
    cots = [Fetched(cotangent.at[r], cot.at[k], sems.at[1 + k]) for k, r in ((0, parity), (1, 1 - parity))]
    states = [Fetched(state.at[r], p.at[0], sems.at[3 + k]) for k, r, p in ((0, parity, outer), (1, 1 - parity, inner))]
    wide[...] = jnp.zeros_like(wide)
    wide[0:2, 0:n] = lines.now()[...].astype(F32)
    for slot, pair, masks in ((0, outer, mask_o), (1, inner, mask_i)):
        cot = cots[slot].now()
        row = parity if slot == 0 else 1 - parity
        is_first = jnp.full((1, C), row, jnp.int32) == 0
        for at in range(0, n, C):
            size = min(C, n - at)
            line = jnp.where(is_first, wide[0:1, at : at + C], wide[1:2, at : at + C])
            tile = jnp.broadcast_to(line, (C, C)).T[:size]
            masks[at : at + size, :] = tile.astype(BF16)
            pair[1, at : at + size, :] = (cot[at : at + size, :].astype(F32) * tile).astype(BF16)
        states[slot].now()
        outs.send(slot)
        outs.send(2 + slot)


def first_kernel(
    flags, partner, outer, inner, halo, mask_i, w1, w2, outs, pre_o, dact_o, fold, spread,
    taps, utaps, fw, ad, y, d, src, dst, wide, wide_dst, row, sems
):
    parity = flags[0]
    n = src.shape[0]
    (inner2,) = outs
    outer, inner, w1, w2 = outer.now(), inner.now(), w1.now(), w2.now()
    halo = halo.now()
    near_forward(parity, (outer[0], inner[0], halo[0]), w1, taps, fw, y)
    pre = Fetched(y.at[:, pl.ds(0, C)], pre_o, sems.at[0])
    near_adjoint(parity, (outer[1], inner[1], halo[1]), w2, utaps, ad, d)
    dact = Fetched(d.at[:, pl.ds(0, C)], dact_o, sems.at[1])
    mask_i = mask_i.now()

    def finish(rows):
        keep = mask_i[rows, :].astype(F32)
        value, slope = gelu_and_slope(y[rows, C:])
        inner2[0, rows, :] = (keep * value).astype(BF16)
        inner2[1, rows, :] = (slope * (keep * d[rows, C:])).astype(BF16)

    over_chunks(n, finish)
    outs.send(0)

    @pl.when(flags[1] != 0)
    def _():
        src[...] = outer[0].astype(F32)
        u = outer[1].astype(F32)
        wide[:, 0:C] = pltpu.roll(u, n - 1, 0)
        wide[:, C : 2 * C] = u
        wide[:, 2 * C :] = pltpu.roll(u, 1, 0)

        def step(i, carry):
            for k in range(8):
                j = i * 8 + k
                at = partner[j]
                dst[pl.ds(j, 1), :] = src[pl.ds(at, 1), :]
                wide_dst[pl.ds(at, 1), :] = wide[pl.ds(j, 1), :]
            return carry

        lax.fori_loop(0, n // 8, step, 0)
        row[...] = dst[...].astype(BF16)
        pltpu.sync_copy(row, fold)
        for b in range(3):
            utaps[:, C * b : C * b + C] = wide_dst[:, C * b : C * b + C].astype(BF16)
        pltpu.sync_copy(utaps.at[:, pl.ds(0, ROW)], spread)

    pre.now()
    dact.now()


def top_copies(top, fold, row, spread, utaps, sems):
    copies = (pltpu.make_async_copy(fold, row, sems.at[0]), pltpu.make_async_copy(spread, utaps, sems.at[1]))

    @pl.when(top != 0)
    def _():
        for copy in copies:
            copy.start()

    return copies


def forward_taps(taps, halo, row, copy, top):
    @pl.when(top == 0)
    def _():
        put_taps(taps, 0, halo[...], False)

    @pl.when(top != 0)
    def _():
        copy.wait()
        put_taps(taps, 0, row[...], False)


def adjoint_taps(utaps, halo, copy, top):
    @pl.when(top == 0)
    def _():
        put_taps(utaps, 0, halo[...], True)

    @pl.when(top != 0)
    def _():
        copy.wait()


def far_kernel(
    flags, halo_s, w1, pre_o, mask_o, halo_g, w2, dact_o, fold, spread, outs, taps, utaps, y, d, row, sems
):
    parity, top = flags[0], flags[1]
    act, dpre = outs[0].at[0], outs[0].at[1]
    copies = top_copies(top, fold, row, spread, utaps, sems)
    halo_s, w1 = halo_s.now(), w1.now()
    forward_taps(taps, halo_s, row, copies[0], top)
    kernel = jnp.concatenate([w1[3 * row_tap(0, parity) + b] for b in range(3)], axis=1)
    y[...] = lax.dot_general(taps[...], kernel, CONTRACT_LAST, preferred_element_type=F32)
    halo_g, w2 = halo_g.now(), w2.now()
    adjoint_taps(utaps, halo_g, copies[1], top)
    a = row_tap(2 - 2 * top, parity)
    kernel = jnp.concatenate([w2[3 * a + b] for b in range(3)], axis=0)
    d[...] = jnp.dot(utaps[...], kernel, preferred_element_type=F32)
    pre_o, dact_o, mask_o = pre_o.now(), dact_o.now(), mask_o.now()

    def step(rows):
        keep = mask_o[rows, :].astype(F32)
        value, slope = gelu_and_slope(pre_o[rows, :] + y[rows, :])
        act[rows, :] = (keep * value).astype(BF16)
        dpre[rows, :] = (slope * (keep * (dact_o[rows, :] + d[rows, :]))).astype(BF16)

    over_chunks(y.shape[0], step)


def weights_kernel(
    flags, partner, outer, inner, halo_in, halo_s, halo_g, outer2, inner2, fold, spread, w1, outs,
    spread2, blank1, blank2, blank3, blank4, blank5, blank6, blank7,
    g1, g2, taps, utaps, htaps, hutaps, row, sems, term, total
):
    parity, top = flags[0], flags[1]
    keep, give = outs
    copies = top_copies(top, fold, row, spread, hutaps, sems)
    for k, pair in enumerate((outer, inner, halo_in)):
        pair = pair.now()
        put_taps(taps, ROW * k, pair[0], False)
        put_taps(utaps, ROW * k, pair[1], True)
    forward_taps(htaps, halo_s.now(), row, copies[0], top)
    adjoint_taps(hutaps, halo_g.now(), copies[1], top)
    outer2, inner2 = outer2.now(), inner2.now()
    act = jnp.concatenate([outer2[0], inner2[0]], axis=1)
    dpre = jnp.concatenate([outer2[1], inner2[1]], axis=1)
    p = lax.dot_general(dpre, taps[...], CONTRACT_ROWS, preferred_element_type=F32)
    q = lax.dot_general(outer2[1], htaps[...], CONTRACT_ROWS, preferred_element_type=F32)
    first, last = row_tap(0, parity), row_tap(2, parity)

    def block(x, r, k, b):
        return x[r * C : r * C + C, ROW * k + C * b : ROW * k + C * b + C]

    for b in range(3):
        g1[3 * first + b] = block(p, INN, OUT, b) + block(q, 0, 0, b)
        g1[3 + b] = block(p, OUT, OUT, b) + block(p, INN, INN, b)
        g1[3 * last + b] = block(p, OUT, INN, b) + block(p, INN, FAR, b)
    p = lax.dot_general(act, utaps[...], CONTRACT_ROWS, preferred_element_type=F32)
    q = lax.dot_general(outer2[0], hutaps[...], CONTRACT_ROWS, preferred_element_type=F32)
    is_top = jnp.full((C, C), top, jnp.int32) != 0
    for b in range(3):
        edge = block(q, 0, 0, b)
        g2[3 * first + b] = (block(p, OUT, INN, b) + block(p, INN, FAR, b) + jnp.where(is_top, edge, 0.0)).T
        g2[3 + b] = (block(p, OUT, OUT, b) + block(p, INN, INN, b)).T
        g2[3 * last + b] = (block(p, INN, OUT, b) + jnp.where(is_top, 0.0, edge)).T
    pairs, _, per, _ = keep.shape
    for here in range(2):

        @pl.when(parity == here)
        def _():
            for which, g in enumerate((g1, g2)):
                for owner in range(2 * pairs):
                    dst = keep if owner % 2 == here else give
                    at = owner * per
                    while at < (owner + 1) * per:
                        t = at // C
                        stop = min((owner + 1) * per, (t + 1) * C)
                        rows = slice(at - owner * per, stop - owner * per)
                        dst[owner // 2, which, rows, :] = g[t, at - t * C : stop - t * C, :]
                        at = stop
    outs.send(0)
    outs.send(1)

    @pl.when(top != 0)
    def _():
        put_taps(hutaps, 0, outer2[1], True)
        pltpu.sync_copy(w1.at[6], htaps.at[pl.ds(0, C), pl.ds(0, C)])
        pltpu.sync_copy(w1.at[7], htaps.at[pl.ds(C, C), pl.ds(0, C)])
        pltpu.sync_copy(w1.at[8], htaps.at[pl.ds(2 * C, C), pl.ds(0, C)])
        term[...] = jnp.dot(hutaps[...], htaps[: 3 * C, :C], preferred_element_type=F32)

        def step(i, carry):
            for k in range(16):
                j = i * 16 + k
                total[pl.ds(partner[j], 1), :] = term[pl.ds(j, 1), :]
            return carry

        lax.fori_loop(0, term.shape[0] // 16, step, 0)
        pltpu.sync_copy(total, spread2)


def second_forward_kernel(
    flags, partner, outer2, inner2, halo, w2, outer, inner, mask_i, outs, fold, taps, fw, y, src, dst, row
):
    upd_i, upd_o = outs
    outer2, inner2, halo, w2 = outer2.now(), inner2.now(), halo.now(), w2.now()
    near_forward(flags[0], (outer2[...], inner2[...], halo[...]), w2, taps, fw, y)
    outer, inner, mask_i = outer.now(), inner.now(), mask_i.now()

    def finish(rows):
        upd_o[rows, :] = outer[rows, :].astype(F32) + y[rows, :C]
        keep = mask_i[rows, :].astype(F32)
        upd_i[rows, :] = (keep * (inner[rows, :].astype(F32) + y[rows, C:])).astype(BF16)

    over_chunks(y.shape[0], finish)
    outs.send(0)
    outs.send(1)

    @pl.when(flags[1] != 0)
    def _():
        src[...] = outer2[...].astype(F32)

        def step(i, carry):
            for k in range(16):
                j = i * 16 + k
                dst[pl.ds(j, 1), :] = src[pl.ds(partner[j], 1), :]
            return carry

        lax.fori_loop(0, src.shape[0] // 16, step, 0)
        row[...] = dst[...].astype(BF16)
        pltpu.sync_copy(row, fold)


def second_adjoint_kernel(flags, outer2, inner2, halo, w1, outer, inner, outs, taps, ad, d):
    grad_i, grad_o = outs
    outer2, inner2, halo, w1 = outer2.now(), inner2.now(), halo.now(), w1.now()
    near_adjoint(flags[0], (outer2[...], inner2[...], halo[...]), w1, taps, ad, d)
    outer, inner = outer.now(), inner.now()

    def finish(rows):
        grad_o[rows, :] = outer[rows, :].astype(F32) + d[rows, :C]
        grad_i[rows, :] = (inner[rows, :].astype(F32) + d[rows, C:]).astype(BF16)

    over_chunks(d.shape[0], finish)


def halve_kernel(which, flags, kept, taken, go, stay):
    mine = flags[which]
    for at in range(kept.shape[0]):
        go[at] = (kept[at, 1 - mine] + taken[at, 1 - mine].astype(F32)).astype(go.dtype)
        stay[at] = kept[at, mine] + taken[at, mine].astype(F32)


def total_kernel(kept, taken, first, second):
    first[...] = kept[0] + taken[0].astype(F32)
    second[...] = kept[1] + taken[1].astype(F32)


def last_kernel(
    flags, halo, w2, w1, upd_o, mask_o, grad_o, upd_i, grad_i, fold, spread, updated, grad,
    taps, utaps, y, d, row, top_sems, out_u, out_g, sems
):
    parity, top = flags[0], flags[1]
    halo, w2 = halo.now(), w2.now()
    sent = []

    def send(src, dst):
        copy = pltpu.make_async_copy(src, dst, sems.at[len(sent)])
        copy.start()
        sent.append(copy)

    copies = top_copies(top, fold, row, spread, d, top_sems)
    forward_taps(taps, halo.at[0], row, copies[0], top)
    kernel = jnp.concatenate([w2[3 * row_tap(0, parity) + b] for b in range(3)], axis=1)
    y[...] = lax.dot_general(taps[...], kernel, CONTRACT_LAST, preferred_element_type=F32)
    w1, upd_o, mask_o = w1.now(), upd_o.now(), mask_o.now()

    def step(rows):
        out_u[rows, :] = (mask_o[rows, :].astype(F32) * (upd_o[rows, :] + y[rows, :])).astype(BF16)

    over_chunks(y.shape[0], step)
    send(out_u, updated.at[parity])
    send(upd_i.now(), updated.at[1 - parity])
    send(grad_i.now(), grad.at[1 - parity])

    @pl.when(top == 0)
    def _():
        put_taps(utaps, 0, halo[1], True)
        kernel = jnp.concatenate([w1[3 * row_tap(2, parity) + b] for b in range(3)], axis=0)
        d[...] = jnp.dot(utaps[...], kernel, preferred_element_type=F32)

    @pl.when(top != 0)
    def _():
        copies[1].wait()

    grad_o = grad_o.now()

    def step(rows):
        out_g[rows, :] = (grad_o[rows, :] + d[rows, :]).astype(BF16)

    over_chunks(y.shape[0], step)
    send(out_g, grad.at[parity])
    for copy in sent:
        copy.wait()


class Sent(tuple):
    def send(self, k):
        if k not in self.started:
            self.copies[k].start()
            self.started.append(k)


def call(kernel, scalars, operands, outs, scratch, limit, name, loose=(), loose_outs=()):
    n_in, n_out = len(operands), len(outs)
    shapes = [x[0].shape[1:] if isinstance(x, tuple) else x.shape for x in operands]
    arrays = [x[0] if isinstance(x, tuple) else x for x in operands]

    def run(*refs):
        refs = list(refs)

        def take(k):
            head = refs[:k]
            del refs[:k]
            return head

        small, given, free, results, free_out = (
            take(k) for k in (len(scalars), n_in, len(loose), n_out, len(loose_outs))
        )
        inside, made, sem_in, sem_out = take(n_in), take(n_out), *take(2)
        given = [g.at[x[1]] if isinstance(x, tuple) else g for g, x in zip(given, operands)]
        fetched = [Fetched(g, v, sem_in.at[k]) for k, (g, v) in enumerate(zip(given, inside))]
        sent = Sent(made)
        sent.started = []
        sent.copies = [pltpu.make_async_copy(v, r, sem_out.at[k]) for k, (v, r) in enumerate(zip(made, results))]
        kernel(*small, *fetched, *free, *([sent] if n_out else []), *free_out, *refs)
        for x in fetched:
            x.now()
        for k in range(n_out):
            sent.send(k)
        for copy in sent.copies:
            copy.wait()

    results = pl.pallas_call(
        run,
        in_specs=[SMEM] * len(scalars) + [HBM] * (n_in + len(loose)),
        out_specs=tuple(HBM for _ in range(n_out + len(loose_outs))),
        out_shape=tuple(outs) + tuple(loose_outs),
        scratch_shapes=[pltpu.VMEM(shape, x.dtype) for shape, x in zip(shapes, arrays)]
        + [pltpu.VMEM(x.shape, x.dtype) for x in outs]
        + [pltpu.SemaphoreType.DMA((max(1, n_in),)), pltpu.SemaphoreType.DMA((max(1, n_out),))]
        + list(scratch),
        compiler_params=pltpu.CompilerParams(vmem_limit_bytes=limit * MiB),
        cost_estimate=pl.CostEstimate(flops=1000, transcendentals=0, bytes_accessed=1000),
        name=name,
    )(*scalars, *arrays, *loose)
    return list(results)


def swap(x, n, inner):
    if inner:
        pairs = [(i, i ^ 1) for i in range(n)]
    else:
        pairs = [(i, i + 1) for i in range(1, n - 1, 2)]
        pairs = pairs + [(j, i) for i, j in pairs]
    return lax.ppermute(x, "lat", pairs)


def on_device(ocean_state, cotangent, land_mask, fold_partner, conv_first, conv_second):
    lat = lax.axis_size("lat")
    index = lax.axis_index("lat")
    n = ocean_state.shape[2]
    assert ocean_state.shape[1] == 2 and lat % 2 == 0
    bits = lat.bit_length() - 1
    parity = index & 1
    top = (index == lat - 1).astype(jnp.int32)
    order = list(range(2, bits)) + ([1] if bits > 1 else [])
    flags = jnp.stack([parity, top] + [(index >> bit) & 1 for bit in order]).astype(jnp.int32)
    row = jax.ShapeDtypeStruct((n, C), BF16)
    wide = jax.ShapeDtypeStruct((n, C), F32)
    pair = jax.ShapeDtypeStruct((2, n, C), BF16)
    taps1 = jax.ShapeDtypeStruct((n, ROW), BF16)
    per = 9 * C // lat
    part = jax.ShapeDtypeStruct((lat // 2, 2, per, C), F32)
    own = jax.ShapeDtypeStruct((per, C), F32)
    row_s, wide_s = pltpu.VMEM((n, C), BF16), pltpu.VMEM((n, C), F32)
    near_s = [pltpu.VMEM((n, 3 * ROW), BF16)] * 2 + [pltpu.VMEM((2 * C, 3 * ROW), BF16), pltpu.VMEM((3 * ROW, 2 * C), BF16)]
    near_s = near_s + [pltpu.VMEM((n, 2 * C), F32)] * 2
    dma = pltpu.SemaphoreType.DMA
    far_s = [pltpu.VMEM((n, ROW), BF16)] * 2 + [wide_s] * 2 + [row_s, dma((2,))]
    padded = pl.cdiv(n, C) * C

    outer, inner, mask_o, mask_i = call(
        start_kernel, (flags,), (), [pair, pair, row, row],
        [pltpu.VMEM((8, padded), F32), pltpu.VMEM((2, n), jnp.int32), pltpu.VMEM((2, n, C), BF16), dma((5,))],
        60, "start", loose=(ocean_state.transpose(1, 2, 0), cotangent.transpose(1, 2, 0), land_mask),
    )
    halo = swap(outer, lat, False)
    halo_in = swap(inner, lat, True)
    inner2, pre_o, dact_o, fold1, spread1 = call(
        first_kernel, (flags, fold_partner), (outer, inner, halo_in, mask_i, conv_first, conv_second), [pair],
        near_s + [wide_s, wide_s, pltpu.VMEM((n, ROW), F32), pltpu.VMEM((n, ROW), F32), row_s, dma((2,))], 60, "first",
        loose_outs=[wide, wide, row, taps1],
    )
    outer2 = call(
        far_kernel, (flags,), ((halo, 0), conv_first, pre_o, mask_o, (halo, 1), conv_second, dact_o), [pair],
        far_s, 60, "far", loose=(fold1, spread1),
    )[0]
    halo2 = swap(outer2, lat, False)
    halo_in2 = swap(inner2, lat, True)
    keep, give, spread2, own1, own2, *blank = call(
        weights_kernel, (flags, fold_partner), (outer, inner, halo_in, (halo, 0), (halo, 1), outer2, inner2), [part, part],
        [pltpu.VMEM((9, C, C), F32)] * 2 + [pltpu.VMEM((n, 3 * ROW), BF16)] * 2
        + [pltpu.VMEM((n, ROW), BF16)] * 2 + [row_s, dma((2,)), wide_s, wide_s], 60, "wgrad",
        loose=(fold1, spread1, conv_first), loose_outs=[wide, own, own, row, wide, row, wide, row],
    )

    def body(carry):
        turn, given, _ = carry
        now = flags + 2 * turn
        arrived = swap(given, lat, True)
        kept, taken = keep, arrived
        params = pltpu.CompilerParams(vmem_limit_bytes=8 * MiB)
        cost = pl.CostEstimate(flops=1000, transcendentals=0, bytes_accessed=1000)
        left = list(range(bits - 1, 0, -1))
        beside = []
        for stage, bit in enumerate(order):
            axis = left.index(bit)
            split = (2**axis, 2, 2 ** (len(left) - axis - 1) * 2, per, C)
            left.pop(axis)
            half = jax.ShapeDtypeStruct(split[:1] + split[2:], F32)
            sent = jax.ShapeDtypeStruct(half.shape, LINKS.get(stage, F32))
            go, kept = pl.pallas_call(
                functools.partial(halve_kernel, 2 + stage), in_specs=[SMEM, VMEM, VMEM], out_specs=(VMEM, VMEM),
                out_shape=(sent, half), compiler_params=params, cost_estimate=cost, name=f"halve{stage}",
            )(now, kept.reshape(split), taken.reshape(split))
            if 1 <= stage <= 2:
                go, beside[stage - 1] = lax.optimization_barrier((go, beside[stage - 1]))
            pairs = [(i, i ^ (1 << bit)) for i in range(lat)]
            taken = lax.ppermute(go, "lat", pairs)
            if stage == 0:
                beside.append(
                    call(
                        second_forward_kernel, (now, fold_partner),
                        ((outer2, 0), (inner2, 0), (halo_in2, 0), conv_second, (outer, 0), (inner, 0), mask_i), [row, wide],
                        near_s[0:1] + near_s[2:3] + near_s[4:5] + [wide_s, wide_s, row_s], 30, "second", loose_outs=[row],
                    )
                )
                beside.append(
                    call(
                        second_adjoint_kernel, (now,),
                        ((outer2, 1), (inner2, 1), (halo_in2, 1), conv_first, (outer, 1), (inner, 1)), [row, wide],
                        near_s[0:1] + near_s[3:4] + near_s[4:5], 28, "second_adjoint",
                    )
                )
        total = pl.pallas_call(
            total_kernel, in_specs=[VMEM, VMEM], out_specs=(VMEM, VMEM), out_shape=(own, own), compiler_params=params,
            cost_estimate=cost, name="total",
        )(kept.reshape(2, per, C), taken.reshape(2, per, C))
        return turn + 1, arrived, (list(total), beside)

    stop = jnp.minimum(1, parity + 1)
    start = ([own1, own2], [[blank[0], blank[1], blank[4]], [blank[2], blank[3]]])
    _, _, ((g1, g2), (near, near_a)) = lax.while_loop(lambda c: c[0] < stop, body, (jnp.int32(0), give, start))
    fold2 = near[2], spread2
    (upd_i, upd_o), (grad_i, grad_o) = near[:2], near_a[:2]
    updated, grad = call(
        last_kernel, (flags,), (halo2, conv_second, conv_first, upd_o, mask_o, grad_o, upd_i, grad_i), [],
        far_s + [row_s, row_s, dma((4,))], 28, "last", loose=tuple(fold2), loose_outs=[pair, pair],
    )
    return (updated.transpose(2, 0, 1), grad.transpose(2, 0, 1), g1, g2)


def solution(mesh):
    placed = (
        P(None, ("rep", "lat"), None),
        P(None, ("rep", "lat"), None),
        P("lat", None),
        P(),
        P(),
        P(),
    )
    return jax.shard_map(
        on_device,
        mesh=mesh,
        in_specs=placed,
        out_specs=(
            P(None, ("rep", "lat"), None),
            P(None, ("rep", "lat"), None),
            P(("rep", "lat"), None),
            P(("rep", "lat"), None),
        ),
        check_vma=False,
    )
```

```python
import functools

import jax
import jax.numpy as jnp
import numpy as np
from jax import lax
from jax.experimental import pallas as pl
from jax.experimental.pallas import tpu as pltpu
from jax.sharding import PartitionSpec as P

C = 128
F32 = jnp.float32
BF16 = jnp.bfloat16
SMEM = pl.BlockSpec(memory_space=pltpu.SMEM)
VMEM = pl.BlockSpec(memory_space=pltpu.VMEM)
HBM = pl.BlockSpec(memory_space=pltpu.HBM)
MiB = 1 << 20
OUT, INN = 0, 1
FAR = 2
ROW = 3 * C
CONTRACT_LAST = (((1,), (1,)), ((), ()))
CONTRACT_ROWS = (((0,), (0,)), ((), ()))
FORWARD = ((OUT, OUT, 1), (OUT, INN, 2), (INN, OUT, 0), (INN, INN, 1), (INN, FAR, 2))
ADJOINT = ((OUT, OUT, 1), (INN, OUT, 2), (OUT, INN, 0), (INN, INN, 1), (INN, FAR, 0))
SCALE = np.float32(np.sqrt(2 / np.pi))
CUBE = np.float32(0.044715)
HALF = np.float32(0.5)
LINKS = {0: BF16, 1: BF16}


def chunk_of(n):
    for size in (432, 400, 384, 320, 256, 240, 144, 128, 80, 64, 48, 32, 16):
        if n % size == 0:
            return size
    return n


def put_taps(dst, at, row, adjoint):
    n = row.shape[0]
    wide = row.astype(F32)
    before = pltpu.roll(wide, 1, 0).astype(BF16)
    after = pltpu.roll(wide, n - 1, 0).astype(BF16)
    taps = (after, row, before) if adjoint else (before, row, after)
    for b, tap in enumerate(taps):
        dst[:, at + C * b : at + C * b + C] = tap


def row_tap(a, parity):
    return a + parity * (2 - 2 * a)


def build_forward(dst, w, parity):
    dst[...] = jnp.zeros_like(dst)
    for ro, ri, a in FORWARD:
        for b in range(3):
            at = ROW * ri + C * b
            dst[ro * C : ro * C + C, at : at + C] = w[3 * row_tap(a, parity) + b]


def build_adjoint(dst, w, parity):
    dst[...] = jnp.zeros_like(dst)
    for ro, ri, a in ADJOINT:
        for b in range(3):
            at = ROW * ri + C * b
            dst[at : at + C, ro * C : ro * C + C] = w[3 * row_tap(a, parity) + b]


def gelu_and_slope(x):
    square = x * x
    t = jnp.tanh(SCALE * (x + CUBE * (x * square)))
    cdf = HALF * (1.0 + t)
    slope = cdf + (HALF * x) * (1.0 - t * t) * (SCALE * (1.0 + np.float32(3) * CUBE * square))
    return x * cdf, slope


def over_chunks(n, step):
    m = chunk_of(n)

    def body(k, carry):
        step(pl.ds(pl.multiple_of(k * m, m), m))
        return carry

    lax.fori_loop(0, n // m, body, 0)


def near_forward(parity, rows, w, taps, fw, y):
    build_forward(fw, w, parity)
    for k in range(3):
        put_taps(taps, ROW * k, rows[k], False)
    y[...] = lax.dot_general(taps[...], fw[...], CONTRACT_LAST, preferred_element_type=F32)


def near_adjoint(parity, rows, w, taps, ad, d):
    build_adjoint(ad, w, parity)
    for k in range(3):
        put_taps(taps, ROW * k, rows[k], True)
    d[...] = jnp.dot(taps[...], ad[...], preferred_element_type=F32)


class Fetched:
    def __init__(self, src, dst, sem):
        self.ref, self.copy, self.done = dst, pltpu.make_async_copy(src, dst, sem), False
        self.copy.start()

    def now(self):
        if not self.done:
            self.copy.wait()
            self.done = True
        return self.ref


def start_kernel(flags, state, cotangent, mask, outs, wide, lines, cot, sems):
    parity = flags[0]
    outer, inner, mask_o, mask_i = outs
    n = outer.shape[1]
    lines = Fetched(mask, lines, sems.at[0])
    cots = [Fetched(cotangent.at[r], cot.at[k], sems.at[1 + k]) for k, r in ((0, parity), (1, 1 - parity))]
    states = [Fetched(state.at[r], p.at[0], sems.at[3 + k]) for k, r, p in ((0, parity, outer), (1, 1 - parity, inner))]
    wide[...] = jnp.zeros_like(wide)
    wide[0:2, 0:n] = lines.now()[...].astype(F32)
    for slot, pair, masks in ((0, outer, mask_o), (1, inner, mask_i)):
        cot = cots[slot].now()
        row = parity if slot == 0 else 1 - parity
        is_first = jnp.full((1, C), row, jnp.int32) == 0
        for at in range(0, n, C):
            size = min(C, n - at)
            line = jnp.where(is_first, wide[0:1, at : at + C], wide[1:2, at : at + C])
            tile = jnp.broadcast_to(line, (C, C)).T[:size]
            masks[at : at + size, :] = tile.astype(BF16)
            pair[1, at : at + size, :] = (cot[at : at + size, :].astype(F32) * tile).astype(BF16)
        states[slot].now()
        outs.send(slot)
        outs.send(2 + slot)


def first_kernel(
    flags, partner, outer, inner, halo, mask_i, w1, w2, outs, pre_o, dact_o, fold, spread,
    taps, utaps, fw, ad, y, d, src, dst, wide, wide_dst, row, sems
):
    parity = flags[0]
    n = src.shape[0]
    (inner2,) = outs
    outer, inner, w1, w2 = outer.now(), inner.now(), w1.now(), w2.now()
    halo = halo.now()
    near_forward(parity, (outer[0], inner[0], halo[0]), w1, taps, fw, y)
    pre = Fetched(y.at[:, pl.ds(0, C)], pre_o, sems.at[0])
    near_adjoint(parity, (outer[1], inner[1], halo[1]), w2, utaps, ad, d)
    dact = Fetched(d.at[:, pl.ds(0, C)], dact_o, sems.at[1])
    mask_i = mask_i.now()

    def finish(rows):
        keep = mask_i[rows, :].astype(F32)
        value, slope = gelu_and_slope(y[rows, C:])
        inner2[0, rows, :] = (keep * value).astype(BF16)
        inner2[1, rows, :] = (slope * (keep * d[rows, C:])).astype(BF16)

    over_chunks(n, finish)
    outs.send(0)

    @pl.when(flags[1] != 0)
    def _():
        src[...] = outer[0].astype(F32)
        u = outer[1].astype(F32)
        wide[:, 0:C] = pltpu.roll(u, n - 1, 0)
        wide[:, C : 2 * C] = u
        wide[:, 2 * C :] = pltpu.roll(u, 1, 0)

        def step(i, carry):
            for k in range(8):
                j = i * 8 + k
                at = partner[j]
                dst[pl.ds(j, 1), :] = src[pl.ds(at, 1), :]
                wide_dst[pl.ds(at, 1), :] = wide[pl.ds(j, 1), :]
            return carry

        lax.fori_loop(0, n // 8, step, 0)
        row[...] = dst[...].astype(BF16)
        pltpu.sync_copy(row, fold)
        for b in range(3):
            utaps[:, C * b : C * b + C] = wide_dst[:, C * b : C * b + C].astype(BF16)
        pltpu.sync_copy(utaps.at[:, pl.ds(0, ROW)], spread)

    pre.now()
    dact.now()


def top_copies(top, fold, row, spread, utaps, sems):
    copies = (pltpu.make_async_copy(fold, row, sems.at[0]), pltpu.make_async_copy(spread, utaps, sems.at[1]))

    @pl.when(top != 0)
    def _():
        for copy in copies:
            copy.start()

    return copies


def forward_taps(taps, halo, row, copy, top):
    @pl.when(top == 0)
    def _():
        put_taps(taps, 0, halo[...], False)

    @pl.when(top != 0)
    def _():
        copy.wait()
        put_taps(taps, 0, row[...], False)


def adjoint_taps(utaps, at, halo, copy, top):
    @pl.when(top == 0)
    def _():
        put_taps(utaps, at, halo[...], True)

    @pl.when(top != 0)
    def _():
        copy.wait()


def build_far(dst, w_f, a_f, w_a, a_a):
    dst[...] = jnp.zeros_like(dst)
    for b in range(3):
        dst[C * b : C * b + C, :C] = w_f[3 * a_f + b].astype(F32).T.astype(BF16)
        dst[ROW + C * b : ROW + C * b + C, C:] = w_a[3 * a_a + b]


def far_kernel(
    flags, halo_s, w1, pre_o, mask_o, halo_g, w2, dact_o, fold, spread, outs, taps, kernels, y, row, sems
):
    parity, top = flags[0], flags[1]
    act, dpre = outs[0].at[0], outs[0].at[1]
    copies = top_copies(top, fold, row, spread, taps.at[:, pl.ds(ROW, ROW)], sems)
    w1, w2 = w1.now(), w2.now()
    build_far(kernels, w1, row_tap(0, parity), w2, row_tap(2 - 2 * top, parity))
    halo_s, halo_g = halo_s.now(), halo_g.now()
    forward_taps(taps, halo_s, row, copies[0], top)
    adjoint_taps(taps, ROW, halo_g, copies[1], top)
    y[...] = jnp.dot(taps[...], kernels[...], preferred_element_type=F32)
    pre_o, dact_o, mask_o = pre_o.now(), dact_o.now(), mask_o.now()

    def step(rows):
        keep = mask_o[rows, :].astype(F32)
        value, slope = gelu_and_slope(pre_o[rows, :] + y[rows, :C])
        act[rows, :] = (keep * value).astype(BF16)
        dpre[rows, :] = (slope * (keep * (dact_o[rows, :] + y[rows, C:]))).astype(BF16)

    over_chunks(y.shape[0], step)


def weights_kernel(
    flags, partner, outer, inner, halo_in, halo_s, halo_g, outer2, inner2, fold, spread, w1, outs,
    spread2, blank1, blank2, blank3, blank4, blank5, blank6, blank7,
    g1, g2, taps, utaps, htaps, hutaps, row, sems, term, total
):
    parity, top = flags[0], flags[1]
    keep, give = outs
    copies = top_copies(top, fold, row, spread, hutaps, sems)
    for k, pair in enumerate((outer, inner, halo_in)):
        pair = pair.now()
        put_taps(taps, ROW * k, pair[0], False)
        put_taps(utaps, ROW * k, pair[1], True)
    forward_taps(htaps, halo_s.now(), row, copies[0], top)
    adjoint_taps(hutaps, 0, halo_g.now(), copies[1], top)
    outer2, inner2 = outer2.now(), inner2.now()
    act = jnp.concatenate([outer2[0], inner2[0]], axis=1)
    dpre = jnp.concatenate([outer2[1], inner2[1]], axis=1)
    p = lax.dot_general(dpre, taps[...], CONTRACT_ROWS, preferred_element_type=F32)
    q = lax.dot_general(outer2[1], htaps[...], CONTRACT_ROWS, preferred_element_type=F32)
    first, last = row_tap(0, parity), row_tap(2, parity)

    def block(x, r, k, b):
        return x[r * C : r * C + C, ROW * k + C * b : ROW * k + C * b + C]

    for b in range(3):
        g1[3 * first + b] = block(p, INN, OUT, b) + block(q, 0, 0, b)
        g1[3 + b] = block(p, OUT, OUT, b) + block(p, INN, INN, b)
        g1[3 * last + b] = block(p, OUT, INN, b) + block(p, INN, FAR, b)
    p = lax.dot_general(act, utaps[...], CONTRACT_ROWS, preferred_element_type=F32)
    q = lax.dot_general(outer2[0], hutaps[...], CONTRACT_ROWS, preferred_element_type=F32)
    is_top = jnp.full((C, C), top, jnp.int32) != 0
    for b in range(3):
        edge = block(q, 0, 0, b)
        g2[3 * first + b] = (block(p, OUT, INN, b) + block(p, INN, FAR, b) + jnp.where(is_top, edge, 0.0)).T
        g2[3 + b] = (block(p, OUT, OUT, b) + block(p, INN, INN, b)).T
        g2[3 * last + b] = (block(p, INN, OUT, b) + jnp.where(is_top, 0.0, edge)).T
    pairs, _, per, _ = keep.shape
    for here in range(2):

        @pl.when(parity == here)
        def _():
            for which, g in enumerate((g1, g2)):
                for owner in range(2 * pairs):
                    dst = keep if owner % 2 == here else give
                    at = owner * per
                    while at < (owner + 1) * per:
                        t = at // C
                        stop = min((owner + 1) * per, (t + 1) * C)
                        rows = slice(at - owner * per, stop - owner * per)
                        dst[owner // 2, which, rows, :] = g[t, at - t * C : stop - t * C, :]
                        at = stop
    outs.send(0)
    outs.send(1)

    @pl.when(top != 0)
    def _():
        put_taps(hutaps, 0, outer2[1], True)
        pltpu.sync_copy(w1.at[6], htaps.at[pl.ds(0, C), pl.ds(0, C)])
        pltpu.sync_copy(w1.at[7], htaps.at[pl.ds(C, C), pl.ds(0, C)])
        pltpu.sync_copy(w1.at[8], htaps.at[pl.ds(2 * C, C), pl.ds(0, C)])
        term[...] = jnp.dot(hutaps[...], htaps[: 3 * C, :C], preferred_element_type=F32)

        def step(i, carry):
            for k in range(16):
                j = i * 16 + k
                total[pl.ds(partner[j], 1), :] = term[pl.ds(j, 1), :]
            return carry

        lax.fori_loop(0, term.shape[0] // 16, step, 0)
        pltpu.sync_copy(total, spread2)


def second_forward_kernel(
    flags, partner, outer2, inner2, halo, w2, outer, inner, mask_i, outs, fold, taps, fw, y, src, dst, row
):
    upd_i, upd_o = outs
    outer2, inner2, halo, w2 = outer2.now(), inner2.now(), halo.now(), w2.now()
    near_forward(flags[0], (outer2[...], inner2[...], halo[...]), w2, taps, fw, y)
    outer, inner, mask_i = outer.now(), inner.now(), mask_i.now()

    def finish(rows):
        upd_o[rows, :] = outer[rows, :].astype(F32) + y[rows, :C]
        keep = mask_i[rows, :].astype(F32)
        upd_i[rows, :] = (keep * (inner[rows, :].astype(F32) + y[rows, C:])).astype(BF16)

    over_chunks(y.shape[0], finish)
    outs.send(0)
    outs.send(1)

    @pl.when(flags[1] != 0)
    def _():
        src[...] = outer2[...].astype(F32)

        def step(i, carry):
            for k in range(16):
                j = i * 16 + k
                dst[pl.ds(j, 1), :] = src[pl.ds(partner[j], 1), :]
            return carry

        lax.fori_loop(0, src.shape[0] // 16, step, 0)
        row[...] = dst[...].astype(BF16)
        pltpu.sync_copy(row, fold)


def second_adjoint_kernel(flags, outer2, inner2, halo, w1, outer, inner, outs, taps, ad, d):
    grad_i, grad_o = outs
    outer2, inner2, halo, w1 = outer2.now(), inner2.now(), halo.now(), w1.now()
    near_adjoint(flags[0], (outer2[...], inner2[...], halo[...]), w1, taps, ad, d)
    outer, inner = outer.now(), inner.now()

    def finish(rows):
        grad_o[rows, :] = outer[rows, :].astype(F32) + d[rows, :C]
        grad_i[rows, :] = (inner[rows, :].astype(F32) + d[rows, C:]).astype(BF16)

    over_chunks(d.shape[0], finish)


def halve_kernel(which, flags, kept, taken, go, stay):
    mine = flags[which]
    for at in range(kept.shape[0]):
        go[at] = (kept[at, 1 - mine] + taken[at, 1 - mine].astype(F32)).astype(go.dtype)
        stay[at] = kept[at, mine] + taken[at, mine].astype(F32)


def total_kernel(kept, taken, first, second):
    first[...] = kept[0] + taken[0].astype(F32)
    second[...] = kept[1] + taken[1].astype(F32)


def last_kernel(
    flags, halo, w2, w1, upd_o, mask_o, grad_o, upd_i, grad_i, fold, spread, updated, grad,
    taps, utaps, y, d, row, top_sems, out_u, out_g, sems
):
    parity, top = flags[0], flags[1]
    halo, w2 = halo.now(), w2.now()
    sent = []

    def send(src, dst):
        copy = pltpu.make_async_copy(src, dst, sems.at[len(sent)])
        copy.start()
        sent.append(copy)

    copies = top_copies(top, fold, row, spread, d, top_sems)
    forward_taps(taps, halo.at[0], row, copies[0], top)
    kernel = jnp.concatenate([w2[3 * row_tap(0, parity) + b] for b in range(3)], axis=1)
    y[...] = lax.dot_general(taps[...], kernel, CONTRACT_LAST, preferred_element_type=F32)
    w1, upd_o, mask_o = w1.now(), upd_o.now(), mask_o.now()

    def step(rows):
        out_u[rows, :] = (mask_o[rows, :].astype(F32) * (upd_o[rows, :] + y[rows, :])).astype(BF16)

    over_chunks(y.shape[0], step)
    send(out_u, updated.at[parity])
    send(upd_i.now(), updated.at[1 - parity])
    send(grad_i.now(), grad.at[1 - parity])

    @pl.when(top == 0)
    def _():
        put_taps(utaps, 0, halo[1], True)
        kernel = jnp.concatenate([w1[3 * row_tap(2, parity) + b] for b in range(3)], axis=0)
        d[...] = jnp.dot(utaps[...], kernel, preferred_element_type=F32)

    @pl.when(top != 0)
    def _():
        copies[1].wait()

    grad_o = grad_o.now()

    def step(rows):
        out_g[rows, :] = (grad_o[rows, :] + d[rows, :]).astype(BF16)

    over_chunks(y.shape[0], step)
    send(out_g, grad.at[parity])
    for copy in sent:
        copy.wait()


class Sent(tuple):
    def send(self, k):
        if k not in self.started:
            self.copies[k].start()
            self.started.append(k)


def call(kernel, scalars, operands, outs, scratch, limit, name, loose=(), loose_outs=()):
    n_in, n_out = len(operands), len(outs)
    shapes = [x[0].shape[1:] if isinstance(x, tuple) else x.shape for x in operands]
    arrays = [x[0] if isinstance(x, tuple) else x for x in operands]

    def run(*refs):
        refs = list(refs)

        def take(k):
            head = refs[:k]
            del refs[:k]
            return head

        small, given, free, results, free_out = (
            take(k) for k in (len(scalars), n_in, len(loose), n_out, len(loose_outs))
        )
        inside, made, sem_in, sem_out = take(n_in), take(n_out), *take(2)
        given = [g.at[x[1]] if isinstance(x, tuple) else g for g, x in zip(given, operands)]
        fetched = [Fetched(g, v, sem_in.at[k]) for k, (g, v) in enumerate(zip(given, inside))]
        sent = Sent(made)
        sent.started = []
        sent.copies = [pltpu.make_async_copy(v, r, sem_out.at[k]) for k, (v, r) in enumerate(zip(made, results))]
        kernel(*small, *fetched, *free, *([sent] if n_out else []), *free_out, *refs)
        for x in fetched:
            x.now()
        for k in range(n_out):
            sent.send(k)
        for copy in sent.copies:
            copy.wait()

    results = pl.pallas_call(
        run,
        in_specs=[SMEM] * len(scalars) + [HBM] * (n_in + len(loose)),
        out_specs=tuple(HBM for _ in range(n_out + len(loose_outs))),
        out_shape=tuple(outs) + tuple(loose_outs),
        scratch_shapes=[pltpu.VMEM(shape, x.dtype) for shape, x in zip(shapes, arrays)]
        + [pltpu.VMEM(x.shape, x.dtype) for x in outs]
        + [pltpu.SemaphoreType.DMA((max(1, n_in),)), pltpu.SemaphoreType.DMA((max(1, n_out),))]
        + list(scratch),
        compiler_params=pltpu.CompilerParams(vmem_limit_bytes=limit * MiB),
        cost_estimate=pl.CostEstimate(flops=1000, transcendentals=0, bytes_accessed=1000),
        name=name,
    )(*scalars, *arrays, *loose)
    return list(results)


def swap(x, n, inner):
    if inner:
        pairs = [(i, i ^ 1) for i in range(n)]
    else:
        pairs = [(i, i + 1) for i in range(1, n - 1, 2)]
        pairs = pairs + [(j, i) for i, j in pairs]
    return lax.ppermute(x, "lat", pairs)


def on_device(ocean_state, cotangent, land_mask, fold_partner, conv_first, conv_second):
    lat = lax.axis_size("lat")
    index = lax.axis_index("lat")
    n = ocean_state.shape[2]
    assert ocean_state.shape[1] == 2 and lat % 2 == 0
    bits = lat.bit_length() - 1
    parity = index & 1
    top = (index == lat - 1).astype(jnp.int32)
    order = list(range(2, bits)) + ([1] if bits > 1 else [])
    flags = jnp.stack([parity, top] + [(index >> bit) & 1 for bit in order]).astype(jnp.int32)
    row = jax.ShapeDtypeStruct((n, C), BF16)
    wide = jax.ShapeDtypeStruct((n, C), F32)
    pair = jax.ShapeDtypeStruct((2, n, C), BF16)
    taps1 = jax.ShapeDtypeStruct((n, ROW), BF16)
    per = 9 * C // lat
    part = jax.ShapeDtypeStruct((lat // 2, 2, per, C), F32)
    own = jax.ShapeDtypeStruct((per, C), F32)
    row_s, wide_s = pltpu.VMEM((n, C), BF16), pltpu.VMEM((n, C), F32)
    near_s = [pltpu.VMEM((n, 3 * ROW), BF16)] * 2 + [pltpu.VMEM((2 * C, 3 * ROW), BF16), pltpu.VMEM((3 * ROW, 2 * C), BF16)]
    near_s = near_s + [pltpu.VMEM((n, 2 * C), F32)] * 2
    dma = pltpu.SemaphoreType.DMA
    far_s = [pltpu.VMEM((n, 2 * ROW), BF16), pltpu.VMEM((2 * ROW, 2 * C), BF16), pltpu.VMEM((n, 2 * C), F32), row_s, dma((2,))]
    padded = pl.cdiv(n, C) * C

    outer, inner, mask_o, mask_i = call(
        start_kernel, (flags,), (), [pair, pair, row, row],
        [pltpu.VMEM((8, padded), F32), pltpu.VMEM((2, n), jnp.int32), pltpu.VMEM((2, n, C), BF16), dma((5,))],
        60, "start", loose=(ocean_state.transpose(1, 2, 0), cotangent.transpose(1, 2, 0), land_mask),
    )
    halo = swap(outer, lat, False)
    halo_in = swap(inner, lat, True)
    inner2, pre_o, dact_o, fold1, spread1 = call(
        first_kernel, (flags, fold_partner), (outer, inner, halo_in, mask_i, conv_first, conv_second), [pair],
        near_s + [wide_s, wide_s, pltpu.VMEM((n, ROW), F32), pltpu.VMEM((n, ROW), F32), row_s, dma((2,))], 60, "first",
        loose_outs=[wide, wide, row, taps1],
    )
    outer2 = call(
        far_kernel, (flags,), ((halo, 0), conv_first, pre_o, mask_o, (halo, 1), conv_second, dact_o), [pair],
        far_s, 60, "far", loose=(fold1, spread1),
    )[0]
    halo2 = swap(outer2, lat, False)
    halo_in2 = swap(inner2, lat, True)
    keep, give, spread2, own1, own2, *blank = call(
        weights_kernel, (flags, fold_partner), (outer, inner, halo_in, (halo, 0), (halo, 1), outer2, inner2), [part, part],
        [pltpu.VMEM((9, C, C), F32)] * 2 + [pltpu.VMEM((n, 3 * ROW), BF16)] * 2
        + [pltpu.VMEM((n, ROW), BF16)] * 2 + [row_s, dma((2,)), wide_s, wide_s], 60, "wgrad",
        loose=(fold1, spread1, conv_first), loose_outs=[wide, own, own, row, wide, row, wide, row],
    )

    def body(carry):
        turn, given, _ = carry
        now = flags + 2 * turn
        arrived = swap(given, lat, True)
        kept, taken = keep, arrived
        params = pltpu.CompilerParams(vmem_limit_bytes=8 * MiB)
        cost = pl.CostEstimate(flops=1000, transcendentals=0, bytes_accessed=1000)
        left = list(range(bits - 1, 0, -1))
        beside = []
        for stage, bit in enumerate(order):
            axis = left.index(bit)
            split = (2**axis, 2, 2 ** (len(left) - axis - 1) * 2, per, C)
            left.pop(axis)
            half = jax.ShapeDtypeStruct(split[:1] + split[2:], F32)
            sent = jax.ShapeDtypeStruct(half.shape, LINKS.get(stage, F32))
            go, kept = pl.pallas_call(
                functools.partial(halve_kernel, 2 + stage), in_specs=[SMEM, VMEM, VMEM], out_specs=(VMEM, VMEM),
                out_shape=(sent, half), compiler_params=params, cost_estimate=cost, name=f"halve{stage}",
            )(now, kept.reshape(split), taken.reshape(split))
            if 1 <= stage <= 2:
                go, beside[stage - 1] = lax.optimization_barrier((go, beside[stage - 1]))
            pairs = [(i, i ^ (1 << bit)) for i in range(lat)]
            taken = lax.ppermute(go, "lat", pairs)
            if stage == 0:
                beside.append(
                    call(
                        second_forward_kernel, (now, fold_partner),
                        ((outer2, 0), (inner2, 0), (halo_in2, 0), conv_second, (outer, 0), (inner, 0), mask_i), [row, wide],
                        near_s[0:1] + near_s[2:3] + near_s[4:5] + [wide_s, wide_s, row_s], 30, "second", loose_outs=[row],
                    )
                )
                beside.append(
                    call(
                        second_adjoint_kernel, (now,),
                        ((outer2, 1), (inner2, 1), (halo_in2, 1), conv_first, (outer, 1), (inner, 1)), [row, wide],
                        near_s[0:1] + near_s[3:4] + near_s[4:5], 28, "second_adjoint",
                    )
                )
        total = pl.pallas_call(
            total_kernel, in_specs=[VMEM, VMEM], out_specs=(VMEM, VMEM), out_shape=(own, own), compiler_params=params,
            cost_estimate=cost, name="total",
        )(kept.reshape(2, per, C), taken.reshape(2, per, C))
        return turn + 1, arrived, (list(total), beside)

    stop = jnp.minimum(1, parity + 1)
    start = ([own1, own2], [[blank[0], blank[1], blank[4]], [blank[2], blank[3]]])
    _, _, ((g1, g2), (near, near_a)) = lax.while_loop(lambda c: c[0] < stop, body, (jnp.int32(0), give, start))
    fold2 = near[2], spread2
    (upd_i, upd_o), (grad_i, grad_o) = near[:2], near_a[:2]
    updated, grad = call(
        last_kernel, (flags,), (halo2, conv_second, conv_first, upd_o, mask_o, grad_o, upd_i, grad_i), [],
        [pltpu.VMEM((n, ROW), BF16)] * 2 + [wide_s] * 2 + [row_s, dma((2,)), row_s, row_s, dma((4,))], 28, "last", loose=tuple(fold2), loose_outs=[pair, pair],
    )
    return (updated.transpose(2, 0, 1), grad.transpose(2, 0, 1), g1, g2)


def solution(mesh):
    placed = (
        P(None, ("rep", "lat"), None),
        P(None, ("rep", "lat"), None),
        P("lat", None),
        P(),
        P(),
        P(),
    )
    return jax.shard_map(
        on_device,
        mesh=mesh,
        in_specs=placed,
        out_specs=(
            P(None, ("rep", "lat"), None),
            P(None, ("rep", "lat"), None),
            P(("rep", "lat"), None),
            P(("rep", "lat"), None),
        ),
        check_vma=False,
    )
```

```python
import functools

import jax
import jax.numpy as jnp
import numpy as np
from jax import lax
from jax.experimental import pallas as pl
from jax.experimental.pallas import tpu as pltpu
from jax.sharding import PartitionSpec as P

C = 128
F32 = jnp.float32
BF16 = jnp.bfloat16
SMEM = pl.BlockSpec(memory_space=pltpu.SMEM)
VMEM = pl.BlockSpec(memory_space=pltpu.VMEM)
HBM = pl.BlockSpec(memory_space=pltpu.HBM)
MiB = 1 << 20
OUT, INN = 0, 1
FAR = 2
BEYOND = 3
ROW = 3 * C
CONTRACT_LAST = (((1,), (1,)), ((), ()))
CONTRACT_ROWS = (((0,), (0,)), ((), ()))
FORWARD = ((OUT, OUT, 1), (OUT, INN, 2), (INN, OUT, 0), (INN, INN, 1), (INN, FAR, 2))
ADJOINT = ((OUT, OUT, 1), (INN, OUT, 2), (OUT, INN, 0), (INN, INN, 1), (INN, FAR, 0))
SCALE = np.float32(np.sqrt(2 / np.pi))
CUBE = np.float32(0.044715)
HALF = np.float32(0.5)
LINKS = {0: BF16, 1: BF16}


def chunk_of(n):
    for size in (432, 400, 384, 320, 256, 240, 144, 128, 80, 64, 48, 32, 16):
        if n % size == 0:
            return size
    return n


def put_taps(dst, at, row, adjoint):
    n = row.shape[0]
    wide = row.astype(F32)
    before = pltpu.roll(wide, 1, 0).astype(BF16)
    after = pltpu.roll(wide, n - 1, 0).astype(BF16)
    taps = (after, row, before) if adjoint else (before, row, after)
    for b, tap in enumerate(taps):
        dst[:, at + C * b : at + C * b + C] = tap


def row_tap(a, parity):
    return a + parity * (2 - 2 * a)


def build_forward(dst, w, parity):
    dst[...] = jnp.zeros_like(dst)
    for ro, ri, a in FORWARD:
        for b in range(3):
            at = ROW * ri + C * b
            dst[ro * C : ro * C + C, at : at + C] = w[3 * row_tap(a, parity) + b]


def build_adjoint(dst, w, parity):
    dst[...] = jnp.zeros_like(dst)
    for ro, ri, a in ADJOINT:
        for b in range(3):
            at = ROW * ri + C * b
            dst[at : at + C, ro * C : ro * C + C] = w[3 * row_tap(a, parity) + b]


def gelu_and_slope(x):
    square = x * x
    t = jnp.tanh(SCALE * (x + CUBE * (x * square)))
    cdf = HALF * (1.0 + t)
    slope = cdf + (HALF * x) * (1.0 - t * t) * (SCALE * (1.0 + np.float32(3) * CUBE * square))
    return x * cdf, slope


def over_chunks(n, step):
    m = chunk_of(n)

    def body(k, carry):
        step(pl.ds(pl.multiple_of(k * m, m), m))
        return carry

    lax.fori_loop(0, n // m, body, 0)


def near_forward(parity, rows, w, taps, fw, y):
    build_forward(fw, w, parity)
    for k in range(3):
        put_taps(taps, ROW * k, rows[k], False)
    y[...] = lax.dot_general(taps[...], fw[...], CONTRACT_LAST, preferred_element_type=F32)


def near_adjoint(parity, rows, w, taps, ad, d):
    build_adjoint(ad, w, parity)
    for k in range(3):
        put_taps(taps, ROW * k, rows[k], True)
    d[...] = jnp.dot(taps[...], ad[...], preferred_element_type=F32)


class Fetched:
    def __init__(self, src, dst, sem):
        self.ref, self.copy, self.done = dst, pltpu.make_async_copy(src, dst, sem), False
        self.copy.start()

    def now(self):
        if not self.done:
            self.copy.wait()
            self.done = True
        return self.ref


def start_kernel(flags, state, cotangent, mask, outs, wide, lines, cot, sems):
    parity = flags[0]
    outer, inner, mask_o, mask_i = outs
    n = outer.shape[1]
    lines = Fetched(mask, lines, sems.at[0])
    cots = [Fetched(cotangent.at[r], cot.at[k], sems.at[1 + k]) for k, r in ((0, parity), (1, 1 - parity))]
    states = [Fetched(state.at[r], p.at[0], sems.at[3 + k]) for k, r, p in ((0, parity, outer), (1, 1 - parity, inner))]
    wide[...] = jnp.zeros_like(wide)
    wide[0:2, 0:n] = lines.now()[...].astype(F32)
    for slot, pair, masks in ((0, outer, mask_o), (1, inner, mask_i)):
        cot = cots[slot].now()
        row = parity if slot == 0 else 1 - parity
        is_first = jnp.full((1, C), row, jnp.int32) == 0
        for at in range(0, n, C):
            size = min(C, n - at)
            line = jnp.where(is_first, wide[0:1, at : at + C], wide[1:2, at : at + C])
            tile = jnp.broadcast_to(line, (C, C)).T[:size]
            masks[at : at + size, :] = tile.astype(BF16)
            pair[1, at : at + size, :] = (cot[at : at + size, :].astype(F32) * tile).astype(BF16)
        states[slot].now()
        outs.send(slot)
        outs.send(2 + slot)


def first_kernel(
    flags, partner, outer, inner, halo, mask_i, w1, w2, outs, pre_o, dact_o, fold, spread,
    taps, utaps, fw, ad, y, d, src, dst, wide, wide_dst, row, sems
):
    parity = flags[0]
    n = src.shape[0]
    (inner2,) = outs
    outer, inner, w1, w2 = outer.now(), inner.now(), w1.now(), w2.now()
    halo = halo.now()
    near_forward(parity, (outer[0], inner[0], halo[0]), w1, taps, fw, y)
    pre = Fetched(y.at[:, pl.ds(0, C)], pre_o, sems.at[0])
    near_adjoint(parity, (outer[1], inner[1], halo[1]), w2, utaps, ad, d)
    dact = Fetched(d.at[:, pl.ds(0, C)], dact_o, sems.at[1])
    mask_i = mask_i.now()

    def finish(rows):
        keep = mask_i[rows, :].astype(F32)
        value, slope = gelu_and_slope(y[rows, C:])
        inner2[0, rows, :] = (keep * value).astype(BF16)
        inner2[1, rows, :] = (slope * (keep * d[rows, C:])).astype(BF16)

    over_chunks(n, finish)
    outs.send(0)

    @pl.when(flags[1] != 0)
    def _():
        src[...] = outer[0].astype(F32)
        u = outer[1].astype(F32)
        wide[:, 0:C] = pltpu.roll(u, n - 1, 0)
        wide[:, C : 2 * C] = u
        wide[:, 2 * C :] = pltpu.roll(u, 1, 0)

        def step(i, carry):
            for k in range(8):
                j = i * 8 + k
                at = partner[j]
                dst[pl.ds(j, 1), :] = src[pl.ds(at, 1), :]
                wide_dst[pl.ds(at, 1), :] = wide[pl.ds(j, 1), :]
            return carry

        lax.fori_loop(0, n // 8, step, 0)
        row[...] = dst[...].astype(BF16)
        pltpu.sync_copy(row, fold)
        for b in range(3):
            utaps[:, C * b : C * b + C] = wide_dst[:, C * b : C * b + C].astype(BF16)
        pltpu.sync_copy(utaps.at[:, pl.ds(0, ROW)], spread)

    pre.now()
    dact.now()


def top_copies(top, fold, row, spread, utaps, sems):
    copies = (pltpu.make_async_copy(fold, row, sems.at[0]), pltpu.make_async_copy(spread, utaps, sems.at[1]))

    @pl.when(top != 0)
    def _():
        for copy in copies:
            copy.start()

    return copies


def forward_taps(taps, halo, row, copy, top, at=0):
    @pl.when(top == 0)
    def _():
        put_taps(taps, at, halo[...], False)

    @pl.when(top != 0)
    def _():
        copy.wait()
        put_taps(taps, at, row[...], False)


def adjoint_taps(utaps, at, halo, copy, top):
    @pl.when(top == 0)
    def _():
        put_taps(utaps, at, halo[...], True)

    @pl.when(top != 0)
    def _():
        copy.wait()


def build_far(dst, w_f, a_f, w_a, a_a):
    dst[...] = jnp.zeros_like(dst)
    for b in range(3):
        dst[C * b : C * b + C, :C] = w_f[3 * a_f + b].astype(F32).T.astype(BF16)
        dst[ROW + C * b : ROW + C * b + C, C:] = w_a[3 * a_a + b]


def far_kernel(
    flags, halo_s, w1, pre_o, mask_o, halo_g, w2, dact_o, fold, spread, outs, taps, kernels, y, row, sems
):
    parity, top = flags[0], flags[1]
    act, dpre = outs[0].at[0], outs[0].at[1]
    copies = top_copies(top, fold, row, spread, taps.at[:, pl.ds(ROW, ROW)], sems)
    w1, w2 = w1.now(), w2.now()
    build_far(kernels, w1, row_tap(0, parity), w2, row_tap(2 - 2 * top, parity))
    halo_s, halo_g = halo_s.now(), halo_g.now()
    forward_taps(taps, halo_s, row, copies[0], top)
    adjoint_taps(taps, ROW, halo_g, copies[1], top)
    y[...] = jnp.dot(taps[...], kernels[...], preferred_element_type=F32)
    pre_o, dact_o, mask_o = pre_o.now(), dact_o.now(), mask_o.now()

    def step(rows):
        keep = mask_o[rows, :].astype(F32)
        value, slope = gelu_and_slope(pre_o[rows, :] + y[rows, :C])
        act[rows, :] = (keep * value).astype(BF16)
        dpre[rows, :] = (slope * (keep * (dact_o[rows, :] + y[rows, C:]))).astype(BF16)

    over_chunks(y.shape[0], step)


def weights_kernel(
    flags, partner, outer, inner, halo_in, halo_s, halo_g, outer2, inner2, fold, spread, w1, outs,
    spread2, blank1, blank2, blank3, blank4, blank5, blank6, blank7,
    g1, g2, taps, utaps, htaps, hutaps, row, sems, term, total
):
    parity, top = flags[0], flags[1]
    keep, give = outs
    copies = top_copies(top, fold, row, spread, utaps.at[:, pl.ds(BEYOND * ROW, ROW)], sems)
    for k, pair in enumerate((outer, inner, halo_in)):
        pair = pair.now()
        put_taps(taps, ROW * k, pair[0], False)
        put_taps(utaps, ROW * k, pair[1], True)
    forward_taps(taps, halo_s.now(), row, copies[0], top, BEYOND * ROW)
    adjoint_taps(utaps, BEYOND * ROW, halo_g.now(), copies[1], top)
    outer2, inner2 = outer2.now(), inner2.now()
    act = jnp.concatenate([outer2[0], inner2[0]], axis=1)
    dpre = jnp.concatenate([outer2[1], inner2[1]], axis=1)
    p = lax.dot_general(dpre, taps[...], CONTRACT_ROWS, preferred_element_type=F32)
    first, last = row_tap(0, parity), row_tap(2, parity)

    def block(x, r, k, b):
        return x[r * C : r * C + C, ROW * k + C * b : ROW * k + C * b + C]

    for b in range(3):
        g1[3 * first + b] = block(p, INN, OUT, b) + block(p, OUT, BEYOND, b)
        g1[3 + b] = block(p, OUT, OUT, b) + block(p, INN, INN, b)
        g1[3 * last + b] = block(p, OUT, INN, b) + block(p, INN, FAR, b)
    p = lax.dot_general(act, utaps[...], CONTRACT_ROWS, preferred_element_type=F32)
    is_top = jnp.full((C, C), top, jnp.int32) != 0
    for b in range(3):
        edge = block(p, OUT, BEYOND, b)
        g2[3 * first + b] = (block(p, OUT, INN, b) + block(p, INN, FAR, b) + jnp.where(is_top, edge, 0.0)).T
        g2[3 + b] = (block(p, OUT, OUT, b) + block(p, INN, INN, b)).T
        g2[3 * last + b] = (block(p, INN, OUT, b) + jnp.where(is_top, 0.0, edge)).T
    pairs, _, per, _ = keep.shape
    for here in range(2):

        @pl.when(parity == here)
        def _():
            for which, g in enumerate((g1, g2)):
                for owner in range(2 * pairs):
                    dst = keep if owner % 2 == here else give
                    at = owner * per
                    while at < (owner + 1) * per:
                        t = at // C
                        stop = min((owner + 1) * per, (t + 1) * C)
                        rows = slice(at - owner * per, stop - owner * per)
                        dst[owner // 2, which, rows, :] = g[t, at - t * C : stop - t * C, :]
                        at = stop
    outs.send(0)
    outs.send(1)

    @pl.when(top != 0)
    def _():
        put_taps(hutaps, 0, outer2[1], True)
        pltpu.sync_copy(w1.at[6], htaps.at[pl.ds(0, C), pl.ds(0, C)])
        pltpu.sync_copy(w1.at[7], htaps.at[pl.ds(C, C), pl.ds(0, C)])
        pltpu.sync_copy(w1.at[8], htaps.at[pl.ds(2 * C, C), pl.ds(0, C)])
        term[...] = jnp.dot(hutaps[...], htaps[: 3 * C, :C], preferred_element_type=F32)

        def step(i, carry):
            for k in range(16):
                j = i * 16 + k
                total[pl.ds(partner[j], 1), :] = term[pl.ds(j, 1), :]
            return carry

        lax.fori_loop(0, term.shape[0] // 16, step, 0)
        pltpu.sync_copy(total, spread2)


def second_forward_kernel(
    flags, partner, outer2, inner2, halo, w2, outer, inner, mask_i, outs, fold, taps, fw, y, src, dst, row
):
    upd_i, upd_o = outs
    outer2, inner2, halo, w2 = outer2.now(), inner2.now(), halo.now(), w2.now()
    near_forward(flags[0], (outer2[...], inner2[...], halo[...]), w2, taps, fw, y)
    outer, inner, mask_i = outer.now(), inner.now(), mask_i.now()

    def finish(rows):
        upd_o[rows, :] = outer[rows, :].astype(F32) + y[rows, :C]
        keep = mask_i[rows, :].astype(F32)
        upd_i[rows, :] = (keep * (inner[rows, :].astype(F32) + y[rows, C:])).astype(BF16)

    over_chunks(y.shape[0], finish)
    outs.send(0)
    outs.send(1)

    @pl.when(flags[1] != 0)
    def _():
        src[...] = outer2[...].astype(F32)

        def step(i, carry):
            for k in range(16):
                j = i * 16 + k
                dst[pl.ds(j, 1), :] = src[pl.ds(partner[j], 1), :]
            return carry

        lax.fori_loop(0, src.shape[0] // 16, step, 0)
        row[...] = dst[...].astype(BF16)
        pltpu.sync_copy(row, fold)


def second_adjoint_kernel(flags, outer2, inner2, halo, w1, outer, inner, outs, taps, ad, d):
    grad_i, grad_o = outs
    outer2, inner2, halo, w1 = outer2.now(), inner2.now(), halo.now(), w1.now()
    near_adjoint(flags[0], (outer2[...], inner2[...], halo[...]), w1, taps, ad, d)
    outer, inner = outer.now(), inner.now()

    def finish(rows):
        grad_o[rows, :] = outer[rows, :].astype(F32) + d[rows, :C]
        grad_i[rows, :] = (inner[rows, :].astype(F32) + d[rows, C:]).astype(BF16)

    over_chunks(d.shape[0], finish)


def halve_kernel(which, flags, kept, taken, go, stay):
    mine = flags[which]
    for at in range(kept.shape[0]):
        go[at] = (kept[at, 1 - mine] + taken[at, 1 - mine].astype(F32)).astype(go.dtype)
        stay[at] = kept[at, mine] + taken[at, mine].astype(F32)


def total_kernel(kept, taken, first, second):
    first[...] = kept[0] + taken[0].astype(F32)
    second[...] = kept[1] + taken[1].astype(F32)


def last_kernel(
    flags, halo, w2, w1, upd_o, mask_o, grad_o, upd_i, grad_i, fold, spread, updated, grad,
    taps, utaps, y, d, row, top_sems, out_u, out_g, sems
):
    parity, top = flags[0], flags[1]
    halo, w2 = halo.now(), w2.now()
    sent = []

    def send(src, dst):
        copy = pltpu.make_async_copy(src, dst, sems.at[len(sent)])
        copy.start()
        sent.append(copy)

    copies = top_copies(top, fold, row, spread, d, top_sems)
    forward_taps(taps, halo.at[0], row, copies[0], top)
    kernel = jnp.concatenate([w2[3 * row_tap(0, parity) + b] for b in range(3)], axis=1)
    y[...] = lax.dot_general(taps[...], kernel, CONTRACT_LAST, preferred_element_type=F32)
    w1, upd_o, mask_o = w1.now(), upd_o.now(), mask_o.now()

    def step(rows):
        out_u[rows, :] = (mask_o[rows, :].astype(F32) * (upd_o[rows, :] + y[rows, :])).astype(BF16)

    over_chunks(y.shape[0], step)
    send(out_u, updated.at[parity])
    send(upd_i.now(), updated.at[1 - parity])
    send(grad_i.now(), grad.at[1 - parity])

    @pl.when(top == 0)
    def _():
        put_taps(utaps, 0, halo[1], True)
        kernel = jnp.concatenate([w1[3 * row_tap(2, parity) + b] for b in range(3)], axis=0)
        d[...] = jnp.dot(utaps[...], kernel, preferred_element_type=F32)

    @pl.when(top != 0)
    def _():
        copies[1].wait()

    grad_o = grad_o.now()

    def step(rows):
        out_g[rows, :] = (grad_o[rows, :] + d[rows, :]).astype(BF16)

    over_chunks(y.shape[0], step)
    send(out_g, grad.at[parity])
    for copy in sent:
        copy.wait()


class Sent(tuple):
    def send(self, k):
        if k not in self.started:
            self.copies[k].start()
            self.started.append(k)


def call(kernel, scalars, operands, outs, scratch, limit, name, loose=(), loose_outs=()):
    n_in, n_out = len(operands), len(outs)
    shapes = [x[0].shape[1:] if isinstance(x, tuple) else x.shape for x in operands]
    arrays = [x[0] if isinstance(x, tuple) else x for x in operands]

    def run(*refs):
        refs = list(refs)

        def take(k):
            head = refs[:k]
            del refs[:k]
            return head

        small, given, free, results, free_out = (
            take(k) for k in (len(scalars), n_in, len(loose), n_out, len(loose_outs))
        )
        inside, made, sem_in, sem_out = take(n_in), take(n_out), *take(2)
        given = [g.at[x[1]] if isinstance(x, tuple) else g for g, x in zip(given, operands)]
        fetched = [Fetched(g, v, sem_in.at[k]) for k, (g, v) in enumerate(zip(given, inside))]
        sent = Sent(made)
        sent.started = []
        sent.copies = [pltpu.make_async_copy(v, r, sem_out.at[k]) for k, (v, r) in enumerate(zip(made, results))]
        kernel(*small, *fetched, *free, *([sent] if n_out else []), *free_out, *refs)
        for x in fetched:
            x.now()
        for k in range(n_out):
            sent.send(k)
        for copy in sent.copies:
            copy.wait()

    results = pl.pallas_call(
        run,
        in_specs=[SMEM] * len(scalars) + [HBM] * (n_in + len(loose)),
        out_specs=tuple(HBM for _ in range(n_out + len(loose_outs))),
        out_shape=tuple(outs) + tuple(loose_outs),
        scratch_shapes=[pltpu.VMEM(shape, x.dtype) for shape, x in zip(shapes, arrays)]
        + [pltpu.VMEM(x.shape, x.dtype) for x in outs]
        + [pltpu.SemaphoreType.DMA((max(1, n_in),)), pltpu.SemaphoreType.DMA((max(1, n_out),))]
        + list(scratch),
        compiler_params=pltpu.CompilerParams(vmem_limit_bytes=limit * MiB),
        cost_estimate=pl.CostEstimate(flops=1000, transcendentals=0, bytes_accessed=1000),
        name=name,
    )(*scalars, *arrays, *loose)
    return list(results)


def swap(x, n, inner):
    if inner:
        pairs = [(i, i ^ 1) for i in range(n)]
    else:
        pairs = [(i, i + 1) for i in range(1, n - 1, 2)]
        pairs = pairs + [(j, i) for i, j in pairs]
    return lax.ppermute(x, "lat", pairs)


def on_device(ocean_state, cotangent, land_mask, fold_partner, conv_first, conv_second):
    lat = lax.axis_size("lat")
    index = lax.axis_index("lat")
    n = ocean_state.shape[2]
    assert ocean_state.shape[1] == 2 and lat % 2 == 0
    bits = lat.bit_length() - 1
    parity = index & 1
    top = (index == lat - 1).astype(jnp.int32)
    order = list(range(2, bits)) + ([1] if bits > 1 else [])
    flags = jnp.stack([parity, top] + [(index >> bit) & 1 for bit in order]).astype(jnp.int32)
    row = jax.ShapeDtypeStruct((n, C), BF16)
    wide = jax.ShapeDtypeStruct((n, C), F32)
    pair = jax.ShapeDtypeStruct((2, n, C), BF16)
    taps1 = jax.ShapeDtypeStruct((n, ROW), BF16)
    per = 9 * C // lat
    part = jax.ShapeDtypeStruct((lat // 2, 2, per, C), F32)
    own = jax.ShapeDtypeStruct((per, C), F32)
    row_s, wide_s = pltpu.VMEM((n, C), BF16), pltpu.VMEM((n, C), F32)
    near_s = [pltpu.VMEM((n, 3 * ROW), BF16)] * 2 + [pltpu.VMEM((2 * C, 3 * ROW), BF16), pltpu.VMEM((3 * ROW, 2 * C), BF16)]
    near_s = near_s + [pltpu.VMEM((n, 2 * C), F32)] * 2
    dma = pltpu.SemaphoreType.DMA
    far_s = [pltpu.VMEM((n, 2 * ROW), BF16), pltpu.VMEM((2 * ROW, 2 * C), BF16), pltpu.VMEM((n, 2 * C), F32), row_s, dma((2,))]
    padded = pl.cdiv(n, C) * C

    outer, inner, mask_o, mask_i = call(
        start_kernel, (flags,), (), [pair, pair, row, row],
        [pltpu.VMEM((8, padded), F32), pltpu.VMEM((2, n), jnp.int32), pltpu.VMEM((2, n, C), BF16), dma((5,))],
        60, "start", loose=(ocean_state.transpose(1, 2, 0), cotangent.transpose(1, 2, 0), land_mask),
    )
    halo = swap(outer, lat, False)
    halo_in = swap(inner, lat, True)
    inner2, pre_o, dact_o, fold1, spread1 = call(
        first_kernel, (flags, fold_partner), (outer, inner, halo_in, mask_i, conv_first, conv_second), [pair],
        near_s + [wide_s, wide_s, pltpu.VMEM((n, ROW), F32), pltpu.VMEM((n, ROW), F32), row_s, dma((2,))], 60, "first",
        loose_outs=[wide, wide, row, taps1],
    )
    outer2 = call(
        far_kernel, (flags,), ((halo, 0), conv_first, pre_o, mask_o, (halo, 1), conv_second, dact_o), [pair],
        far_s, 60, "far", loose=(fold1, spread1),
    )[0]
    halo2 = swap(outer2, lat, False)
    halo_in2 = swap(inner2, lat, True)
    keep, give, spread2, own1, own2, *blank = call(
        weights_kernel, (flags, fold_partner), (outer, inner, halo_in, (halo, 0), (halo, 1), outer2, inner2), [part, part],
        [pltpu.VMEM((9, C, C), F32)] * 2 + [pltpu.VMEM((n, 4 * ROW), BF16)] * 2
        + [pltpu.VMEM((n, ROW), BF16)] * 2 + [row_s, dma((2,)), wide_s, wide_s], 60, "wgrad",
        loose=(fold1, spread1, conv_first), loose_outs=[wide, own, own, row, wide, row, wide, row],
    )

    def body(carry):
        turn, given, _ = carry
        now = flags + 2 * turn
        arrived = swap(given, lat, True)
        kept, taken = keep, arrived
        params = pltpu.CompilerParams(vmem_limit_bytes=8 * MiB)
        cost = pl.CostEstimate(flops=1000, transcendentals=0, bytes_accessed=1000)
        left = list(range(bits - 1, 0, -1))
        beside = []
        for stage, bit in enumerate(order):
            axis = left.index(bit)
            split = (2**axis, 2, 2 ** (len(left) - axis - 1) * 2, per, C)
            left.pop(axis)
            half = jax.ShapeDtypeStruct(split[:1] + split[2:], F32)
            sent = jax.ShapeDtypeStruct(half.shape, LINKS.get(stage, F32))
            go, kept = pl.pallas_call(
                functools.partial(halve_kernel, 2 + stage), in_specs=[SMEM, VMEM, VMEM], out_specs=(VMEM, VMEM),
                out_shape=(sent, half), compiler_params=params, cost_estimate=cost, name=f"halve{stage}",
            )(now, kept.reshape(split), taken.reshape(split))
            if 1 <= stage <= 2:
                go, beside[stage - 1] = lax.optimization_barrier((go, beside[stage - 1]))
            pairs = [(i, i ^ (1 << bit)) for i in range(lat)]
            taken = lax.ppermute(go, "lat", pairs)
            if stage == 0:
                beside.append(
                    call(
                        second_forward_kernel, (now, fold_partner),
                        ((outer2, 0), (inner2, 0), (halo_in2, 0), conv_second, (outer, 0), (inner, 0), mask_i), [row, wide],
                        near_s[0:1] + near_s[2:3] + near_s[4:5] + [wide_s, wide_s, row_s], 30, "second", loose_outs=[row],
                    )
                )
                beside.append(
                    call(
                        second_adjoint_kernel, (now,),
                        ((outer2, 1), (inner2, 1), (halo_in2, 1), conv_first, (outer, 1), (inner, 1)), [row, wide],
                        near_s[0:1] + near_s[3:4] + near_s[4:5], 28, "second_adjoint",
                    )
                )
        total = pl.pallas_call(
            total_kernel, in_specs=[VMEM, VMEM], out_specs=(VMEM, VMEM), out_shape=(own, own), compiler_params=params,
            cost_estimate=cost, name="total",
        )(kept.reshape(2, per, C), taken.reshape(2, per, C))
        return turn + 1, arrived, (list(total), beside)

    stop = jnp.minimum(1, parity + 1)
    start = ([own1, own2], [[blank[0], blank[1], blank[4]], [blank[2], blank[3]]])
    _, _, ((g1, g2), (near, near_a)) = lax.while_loop(lambda c: c[0] < stop, body, (jnp.int32(0), give, start))
    fold2 = near[2], spread2
    (upd_i, upd_o), (grad_i, grad_o) = near[:2], near_a[:2]
    updated, grad = call(
        last_kernel, (flags,), (halo2, conv_second, conv_first, upd_o, mask_o, grad_o, upd_i, grad_i), [],
        [pltpu.VMEM((n, ROW), BF16)] * 2 + [wide_s] * 2 + [row_s, dma((2,)), row_s, row_s, dma((4,))], 28, "last", loose=tuple(fold2), loose_outs=[pair, pair],
    )
    return (updated.transpose(2, 0, 1), grad.transpose(2, 0, 1), g1, g2)


def solution(mesh):
    placed = (
        P(None, ("rep", "lat"), None),
        P(None, ("rep", "lat"), None),
        P("lat", None),
        P(),
        P(),
        P(),
    )
    return jax.shard_map(
        on_device,
        mesh=mesh,
        in_specs=placed,
        out_specs=(
            P(None, ("rep", "lat"), None),
            P(None, ("rep", "lat"), None),
            P(("rep", "lat"), None),
            P(("rep", "lat"), None),
        ),
        check_vma=False,
    )
```

```python
import functools

import jax
import jax.numpy as jnp
import numpy as np
from jax import lax
from jax.experimental import pallas as pl
from jax.experimental.pallas import tpu as pltpu
from jax.sharding import PartitionSpec as P

C = 128
F32 = jnp.float32
BF16 = jnp.bfloat16
SMEM = pl.BlockSpec(memory_space=pltpu.SMEM)
VMEM = pl.BlockSpec(memory_space=pltpu.VMEM)
HBM = pl.BlockSpec(memory_space=pltpu.HBM)
MiB = 1 << 20
OUT, INN = 0, 1
FAR = 2
ROW = 3 * C
CONTRACT_LAST = (((1,), (1,)), ((), ()))
CONTRACT_ROWS = (((0,), (0,)), ((), ()))
FORWARD = ((OUT, OUT, 1), (OUT, INN, 2), (INN, OUT, 0), (INN, INN, 1), (INN, FAR, 2))
ADJOINT = ((OUT, OUT, 1), (INN, OUT, 2), (OUT, INN, 0), (INN, INN, 1), (INN, FAR, 0))
SCALE = np.float32(np.sqrt(2 / np.pi))
CUBE = np.float32(0.044715)
HALF = np.float32(0.5)
LINKS = {0: BF16, 1: BF16}


def chunk_of(n):
    for size in (432, 400, 384, 320, 256, 240, 144, 128, 80, 64, 48, 32, 16):
        if n % size == 0:
            return size
    return n


def put_taps(dst, at, row, adjoint):
    n = row.shape[0]
    wide = row.astype(F32)
    before = pltpu.roll(wide, 1, 0).astype(BF16)
    after = pltpu.roll(wide, n - 1, 0).astype(BF16)
    taps = (after, row, before) if adjoint else (before, row, after)
    for b, tap in enumerate(taps):
        dst[:, at + C * b : at + C * b + C] = tap


def row_tap(a, parity):
    return a + parity * (2 - 2 * a)


def build_forward(dst, w, parity):
    dst[...] = jnp.zeros_like(dst)
    for ro, ri, a in FORWARD:
        for b in range(3):
            at = ROW * ri + C * b
            dst[ro * C : ro * C + C, at : at + C] = w[3 * row_tap(a, parity) + b]


def build_adjoint(dst, w, parity):
    dst[...] = jnp.zeros_like(dst)
    for ro, ri, a in ADJOINT:
        for b in range(3):
            at = ROW * ri + C * b
            dst[at : at + C, ro * C : ro * C + C] = w[3 * row_tap(a, parity) + b]


def gelu_and_slope(x):
    square = x * x
    t = jnp.tanh(SCALE * (x + CUBE * (x * square)))
    cdf = HALF * (1.0 + t)
    slope = cdf + (HALF * x) * (1.0 - t * t) * (SCALE * (1.0 + np.float32(3) * CUBE * square))
    return x * cdf, slope


def over_chunks(n, step):
    m = chunk_of(n)

    def body(k, carry):
        step(pl.ds(pl.multiple_of(k * m, m), m))
        return carry

    lax.fori_loop(0, n // m, body, 0)


def near_forward(parity, rows, w, taps, fw, y):
    build_forward(fw, w, parity)
    for k in range(3):
        put_taps(taps, ROW * k, rows[k], False)
    y[...] = lax.dot_general(taps[...], fw[...], CONTRACT_LAST, preferred_element_type=F32)


def near_adjoint(parity, rows, w, taps, ad, d):
    build_adjoint(ad, w, parity)
    for k in range(3):
        put_taps(taps, ROW * k, rows[k], True)
    d[...] = jnp.dot(taps[...], ad[...], preferred_element_type=F32)


class Fetched:
    def __init__(self, src, dst, sem):
        self.ref, self.copy, self.done = dst, pltpu.make_async_copy(src, dst, sem), False
        self.copy.start()

    def now(self):
        if not self.done:
            self.copy.wait()
            self.done = True
        return self.ref


def start_kernel(flags, state, cotangent, mask, outs, wide, lines, cot, sems):
    parity = flags[0]
    outer, inner, mask_o, mask_i = outs
    n = outer.shape[1]
    lines = Fetched(mask, lines, sems.at[0])
    cots = [Fetched(cotangent.at[r], cot.at[k], sems.at[1 + k]) for k, r in ((0, parity), (1, 1 - parity))]
    states = [Fetched(state.at[r], p.at[0], sems.at[3 + k]) for k, r, p in ((0, parity, outer), (1, 1 - parity, inner))]
    wide[...] = jnp.zeros_like(wide)
    wide[0:2, 0:n] = lines.now()[...].astype(F32)
    for slot, pair, masks in ((0, outer, mask_o), (1, inner, mask_i)):
        cot = cots[slot].now()
        row = parity if slot == 0 else 1 - parity
        is_first = jnp.full((1, C), row, jnp.int32) == 0
        for at in range(0, n, C):
            size = min(C, n - at)
            line = jnp.where(is_first, wide[0:1, at : at + C], wide[1:2, at : at + C])
            tile = jnp.broadcast_to(line, (C, C)).T[:size]
            masks[at : at + size, :] = tile.astype(BF16)
            pair[1, at : at + size, :] = (cot[at : at + size, :].astype(F32) * tile).astype(BF16)
        states[slot].now()
        outs.send(slot)
        outs.send(2 + slot)


def first_kernel(
    flags, partner, outer, inner, halo, mask_i, w1, w2, outs, pre_o, dact_o, fold, spread,
    taps, utaps, fw, ad, y, d, src, dst, wide, wide_dst, row, sems
):
    parity = flags[0]
    n = src.shape[0]
    (inner2,) = outs
    outer, inner, w1, w2 = outer.now(), inner.now(), w1.now(), w2.now()
    halo = halo.now()
    near_forward(parity, (outer[0], inner[0], halo[0]), w1, taps, fw, y)
    pre = Fetched(y.at[:, pl.ds(0, C)], pre_o, sems.at[0])
    near_adjoint(parity, (outer[1], inner[1], halo[1]), w2, utaps, ad, d)
    dact = Fetched(d.at[:, pl.ds(0, C)], dact_o, sems.at[1])
    mask_i = mask_i.now()

    def finish(rows):
        keep = mask_i[rows, :].astype(F32)
        value, slope = gelu_and_slope(y[rows, C:])
        inner2[0, rows, :] = (keep * value).astype(BF16)
        inner2[1, rows, :] = (slope * (keep * d[rows, C:])).astype(BF16)

    over_chunks(n, finish)
    outs.send(0)

    @pl.when(flags[1] != 0)
    def _():
        src[...] = outer[0].astype(F32)
        u = outer[1].astype(F32)
        wide[:, 0:C] = pltpu.roll(u, n - 1, 0)
        wide[:, C : 2 * C] = u
        wide[:, 2 * C :] = pltpu.roll(u, 1, 0)

        def step(i, carry):
            for k in range(16):
                j = i * 16 + k
                at = partner[j]
                dst[pl.ds(j, 1), :] = src[pl.ds(at, 1), :]
                wide_dst[pl.ds(at, 1), :] = wide[pl.ds(j, 1), :]
            return carry

        lax.fori_loop(0, n // 16, step, 0)
        row[...] = dst[...].astype(BF16)
        pltpu.sync_copy(row, fold)
        for b in range(3):
            utaps[:, C * b : C * b + C] = wide_dst[:, C * b : C * b + C].astype(BF16)
        pltpu.sync_copy(utaps.at[:, pl.ds(0, ROW)], spread)

    pre.now()
    dact.now()


def top_copies(top, fold, row, spread, utaps, sems):
    copies = (pltpu.make_async_copy(fold, row, sems.at[0]), pltpu.make_async_copy(spread, utaps, sems.at[1]))

    @pl.when(top != 0)
    def _():
        for copy in copies:
            copy.start()

    return copies


def forward_taps(taps, halo, row, copy, top):
    @pl.when(top == 0)
    def _():
        put_taps(taps, 0, halo[...], False)

    @pl.when(top != 0)
    def _():
        copy.wait()
        put_taps(taps, 0, row[...], False)


def adjoint_taps(utaps, at, halo, copy, top):
    @pl.when(top == 0)
    def _():
        put_taps(utaps, at, halo[...], True)

    @pl.when(top != 0)
    def _():
        copy.wait()


def build_far(dst, w_f, a_f, w_a, a_a):
    dst[...] = jnp.zeros_like(dst)
    for b in range(3):
        dst[C * b : C * b + C, :C] = w_f[3 * a_f + b].astype(F32).T.astype(BF16)
        dst[ROW + C * b : ROW + C * b + C, C:] = w_a[3 * a_a + b]


def far_kernel(
    flags, halo_s, w1, pre_o, mask_o, halo_g, w2, dact_o, fold, spread, outs, taps, kernels, y, row, sems
):
    parity, top = flags[0], flags[1]
    act, dpre = outs[0].at[0], outs[0].at[1]
    copies = top_copies(top, fold, row, spread, taps.at[:, pl.ds(ROW, ROW)], sems)
    w1, w2 = w1.now(), w2.now()
    build_far(kernels, w1, row_tap(0, parity), w2, row_tap(2 - 2 * top, parity))
    halo_s, halo_g = halo_s.now(), halo_g.now()
    forward_taps(taps, halo_s, row, copies[0], top)
    adjoint_taps(taps, ROW, halo_g, copies[1], top)
    y[...] = jnp.dot(taps[...], kernels[...], preferred_element_type=F32)
    pre_o, dact_o, mask_o = pre_o.now(), dact_o.now(), mask_o.now()

    def step(rows):
        keep = mask_o[rows, :].astype(F32)
        value, slope = gelu_and_slope(pre_o[rows, :] + y[rows, :C])
        act[rows, :] = (keep * value).astype(BF16)
        dpre[rows, :] = (slope * (keep * (dact_o[rows, :] + y[rows, C:]))).astype(BF16)

    over_chunks(y.shape[0], step)


def weights_kernel(
    flags, partner, outer, inner, halo_in, halo_s, halo_g, outer2, inner2, fold, spread, w1, outs,
    spread2, blank1, blank2, blank3, blank4, blank5, blank6, blank7,
    g1, g2, taps, utaps, htaps, hutaps, row, sems, term, total
):
    parity, top = flags[0], flags[1]
    keep, give = outs
    copies = top_copies(top, fold, row, spread, hutaps, sems)
    for k, pair in enumerate((outer, inner, halo_in)):
        pair = pair.now()
        put_taps(taps, ROW * k, pair[0], False)
        put_taps(utaps, ROW * k, pair[1], True)
    forward_taps(htaps, halo_s.now(), row, copies[0], top)
    adjoint_taps(hutaps, 0, halo_g.now(), copies[1], top)
    outer2, inner2 = outer2.now(), inner2.now()
    act = jnp.concatenate([outer2[0], inner2[0]], axis=1)
    dpre = jnp.concatenate([outer2[1], inner2[1]], axis=1)
    p = lax.dot_general(dpre, taps[...], CONTRACT_ROWS, preferred_element_type=F32)
    q = lax.dot_general(outer2[1], htaps[...], CONTRACT_ROWS, preferred_element_type=F32)
    first, last = row_tap(0, parity), row_tap(2, parity)

    def block(x, r, k, b):
        return x[r * C : r * C + C, ROW * k + C * b : ROW * k + C * b + C]

    for b in range(3):
        g1[3 * first + b] = block(p, INN, OUT, b) + block(q, 0, 0, b)
        g1[3 + b] = block(p, OUT, OUT, b) + block(p, INN, INN, b)
        g1[3 * last + b] = block(p, OUT, INN, b) + block(p, INN, FAR, b)
    p = lax.dot_general(act, utaps[...], CONTRACT_ROWS, preferred_element_type=F32)
    q = lax.dot_general(outer2[0], hutaps[...], CONTRACT_ROWS, preferred_element_type=F32)
    is_top = jnp.full((C, C), top, jnp.int32) != 0
    for b in range(3):
        edge = block(q, 0, 0, b)
        g2[3 * first + b] = (block(p, OUT, INN, b) + block(p, INN, FAR, b) + jnp.where(is_top, edge, 0.0)).T
        g2[3 + b] = (block(p, OUT, OUT, b) + block(p, INN, INN, b)).T
        g2[3 * last + b] = (block(p, INN, OUT, b) + jnp.where(is_top, 0.0, edge)).T
    pairs, _, per, _ = keep.shape
    for here in range(2):

        @pl.when(parity == here)
        def _():
            for which, g in enumerate((g1, g2)):
                for owner in range(2 * pairs):
                    dst = keep if owner % 2 == here else give
                    at = owner * per
                    while at < (owner + 1) * per:
                        t = at // C
                        stop = min((owner + 1) * per, (t + 1) * C)
                        rows = slice(at - owner * per, stop - owner * per)
                        dst[owner // 2, which, rows, :] = g[t, at - t * C : stop - t * C, :]
                        at = stop
    outs.send(0)
    outs.send(1)

    @pl.when(top != 0)
    def _():
        put_taps(hutaps, 0, outer2[1], True)
        pltpu.sync_copy(w1.at[6], htaps.at[pl.ds(0, C), pl.ds(0, C)])
        pltpu.sync_copy(w1.at[7], htaps.at[pl.ds(C, C), pl.ds(0, C)])
        pltpu.sync_copy(w1.at[8], htaps.at[pl.ds(2 * C, C), pl.ds(0, C)])
        term[...] = jnp.dot(hutaps[...], htaps[: 3 * C, :C], preferred_element_type=F32)

        def step(i, carry):
            for k in range(16):
                j = i * 16 + k
                total[pl.ds(partner[j], 1), :] = term[pl.ds(j, 1), :]
            return carry

        lax.fori_loop(0, term.shape[0] // 16, step, 0)
        pltpu.sync_copy(total, spread2)


def second_forward_kernel(
    flags, partner, outer2, inner2, halo, w2, outer, inner, mask_i, outs, fold, taps, fw, y, src, dst, row
):
    upd_i, upd_o = outs
    outer2, inner2, halo, w2 = outer2.now(), inner2.now(), halo.now(), w2.now()
    near_forward(flags[0], (outer2[...], inner2[...], halo[...]), w2, taps, fw, y)
    outer, inner, mask_i = outer.now(), inner.now(), mask_i.now()

    def finish(rows):
        upd_o[rows, :] = outer[rows, :].astype(F32) + y[rows, :C]
        keep = mask_i[rows, :].astype(F32)
        upd_i[rows, :] = (keep * (inner[rows, :].astype(F32) + y[rows, C:])).astype(BF16)

    over_chunks(y.shape[0], finish)
    outs.send(0)
    outs.send(1)

    @pl.when(flags[1] != 0)
    def _():
        src[...] = outer2[...].astype(F32)

        def step(i, carry):
            for k in range(16):
                j = i * 16 + k
                dst[pl.ds(j, 1), :] = src[pl.ds(partner[j], 1), :]
            return carry

        lax.fori_loop(0, src.shape[0] // 16, step, 0)
        row[...] = dst[...].astype(BF16)
        pltpu.sync_copy(row, fold)


def second_adjoint_kernel(flags, outer2, inner2, halo, w1, outer, inner, outs, taps, ad, d):
    grad_i, grad_o = outs
    outer2, inner2, halo, w1 = outer2.now(), inner2.now(), halo.now(), w1.now()
    near_adjoint(flags[0], (outer2[...], inner2[...], halo[...]), w1, taps, ad, d)
    outer, inner = outer.now(), inner.now()

    def finish(rows):
        grad_o[rows, :] = outer[rows, :].astype(F32) + d[rows, :C]
        grad_i[rows, :] = (inner[rows, :].astype(F32) + d[rows, C:]).astype(BF16)

    over_chunks(d.shape[0], finish)


def halve_kernel(which, flags, kept, taken, go, stay):
    mine = flags[which]
    for at in range(kept.shape[0]):
        go[at] = (kept[at, 1 - mine] + taken[at, 1 - mine].astype(F32)).astype(go.dtype)
        stay[at] = kept[at, mine] + taken[at, mine].astype(F32)


def total_kernel(kept, taken, first, second):
    first[...] = kept[0] + taken[0].astype(F32)
    second[...] = kept[1] + taken[1].astype(F32)


def last_kernel(
    flags, halo, w2, upd_o, mask_o, uhalo, w1, grad_o, upd_i, grad_i, fold, spread, updated, grad,
    taps, utaps, y, d, row, top_sems, out_u, out_g, sems
):
    parity, top = flags[0], flags[1]
    halo, w2 = halo.now(), w2.now()
    sent = []

    def send(src, dst):
        copy = pltpu.make_async_copy(src, dst, sems.at[len(sent)])
        copy.start()
        sent.append(copy)

    copies = top_copies(top, fold, row, spread, d, top_sems)
    forward_taps(taps, halo, row, copies[0], top)
    kernel = jnp.concatenate([w2[3 * row_tap(0, parity) + b] for b in range(3)], axis=1)
    y[...] = lax.dot_general(taps[...], kernel, CONTRACT_LAST, preferred_element_type=F32)
    upd_o, mask_o = upd_o.now(), mask_o.now()

    def step(rows):
        out_u[rows, :] = (mask_o[rows, :].astype(F32) * (upd_o[rows, :] + y[rows, :])).astype(BF16)

    over_chunks(y.shape[0], step)
    send(out_u, updated.at[parity])
    send(upd_i.now(), updated.at[1 - parity])
    send(grad_i.now(), grad.at[1 - parity])
    uhalo, w1 = uhalo.now(), w1.now()

    @pl.when(top == 0)
    def _():
        put_taps(utaps, 0, uhalo[...], True)
        kernel = jnp.concatenate([w1[3 * row_tap(2, parity) + b] for b in range(3)], axis=0)
        d[...] = jnp.dot(utaps[...], kernel, preferred_element_type=F32)

    @pl.when(top != 0)
    def _():
        copies[1].wait()

    grad_o = grad_o.now()

    def step(rows):
        out_g[rows, :] = (grad_o[rows, :] + d[rows, :]).astype(BF16)

    over_chunks(y.shape[0], step)
    send(out_g, grad.at[parity])
    for copy in sent:
        copy.wait()


class Sent(tuple):
    def send(self, k):
        if k not in self.started:
            self.copies[k].start()
            self.started.append(k)


def call(kernel, scalars, operands, outs, scratch, limit, name, loose=(), loose_outs=()):
    n_in, n_out = len(operands), len(outs)
    shapes = [x[0].shape[1:] if isinstance(x, tuple) else x.shape for x in operands]
    arrays = [x[0] if isinstance(x, tuple) else x for x in operands]

    def run(*refs):
        refs = list(refs)

        def take(k):
            head = refs[:k]
            del refs[:k]
            return head

        small, given, free, results, free_out = (
            take(k) for k in (len(scalars), n_in, len(loose), n_out, len(loose_outs))
        )
        inside, made, sem_in, sem_out = take(n_in), take(n_out), *take(2)
        given = [g.at[x[1]] if isinstance(x, tuple) else g for g, x in zip(given, operands)]
        fetched = [Fetched(g, v, sem_in.at[k]) for k, (g, v) in enumerate(zip(given, inside))]
        sent = Sent(made)
        sent.started = []
        sent.copies = [pltpu.make_async_copy(v, r, sem_out.at[k]) for k, (v, r) in enumerate(zip(made, results))]
        kernel(*small, *fetched, *free, *([sent] if n_out else []), *free_out, *refs)
        for x in fetched:
            x.now()
        for k in range(n_out):
            sent.send(k)
        for copy in sent.copies:
            copy.wait()

    results = pl.pallas_call(
        run,
        in_specs=[SMEM] * len(scalars) + [HBM] * (n_in + len(loose)),
        out_specs=tuple(HBM for _ in range(n_out + len(loose_outs))),
        out_shape=tuple(outs) + tuple(loose_outs),
        scratch_shapes=[pltpu.VMEM(shape, x.dtype) for shape, x in zip(shapes, arrays)]
        + [pltpu.VMEM(x.shape, x.dtype) for x in outs]
        + [pltpu.SemaphoreType.DMA((max(1, n_in),)), pltpu.SemaphoreType.DMA((max(1, n_out),))]
        + list(scratch),
        compiler_params=pltpu.CompilerParams(vmem_limit_bytes=limit * MiB),
        cost_estimate=pl.CostEstimate(flops=1000, transcendentals=0, bytes_accessed=1000),
        name=name,
    )(*scalars, *arrays, *loose)
    return list(results)


def swap(x, n, inner):
    if inner:
        pairs = [(i, i ^ 1) for i in range(n)]
    else:
        pairs = [(i, i + 1) for i in range(1, n - 1, 2)]
        pairs = pairs + [(j, i) for i, j in pairs]
    return lax.ppermute(x, "lat", pairs)


def on_device(ocean_state, cotangent, land_mask, fold_partner, conv_first, conv_second):
    lat = lax.axis_size("lat")
    index = lax.axis_index("lat")
    n = ocean_state.shape[2]
    assert ocean_state.shape[1] == 2 and lat % 2 == 0
    bits = lat.bit_length() - 1
    parity = index & 1
    top = (index == lat - 1).astype(jnp.int32)
    order = list(range(2, bits)) + ([1] if bits > 1 else [])
    flags = jnp.stack([parity, top] + [(index >> bit) & 1 for bit in order]).astype(jnp.int32)
    row = jax.ShapeDtypeStruct((n, C), BF16)
    wide = jax.ShapeDtypeStruct((n, C), F32)
    pair = jax.ShapeDtypeStruct((2, n, C), BF16)
    taps1 = jax.ShapeDtypeStruct((n, ROW), BF16)
    per = 9 * C // lat
    part = jax.ShapeDtypeStruct((lat // 2, 2, per, C), F32)
    own = jax.ShapeDtypeStruct((per, C), F32)
    row_s, wide_s = pltpu.VMEM((n, C), BF16), pltpu.VMEM((n, C), F32)
    near_s = [pltpu.VMEM((n, 3 * ROW), BF16)] * 2 + [pltpu.VMEM((2 * C, 3 * ROW), BF16), pltpu.VMEM((3 * ROW, 2 * C), BF16)]
    near_s = near_s + [pltpu.VMEM((n, 2 * C), F32)] * 2
    dma = pltpu.SemaphoreType.DMA
    far_s = [pltpu.VMEM((n, 2 * ROW), BF16), pltpu.VMEM((2 * ROW, 2 * C), BF16), pltpu.VMEM((n, 2 * C), F32), row_s, dma((2,))]
    padded = pl.cdiv(n, C) * C

    outer, inner, mask_o, mask_i = call(
        start_kernel, (flags,), (), [pair, pair, row, row],
        [pltpu.VMEM((8, padded), F32), pltpu.VMEM((2, n), jnp.int32), pltpu.VMEM((2, n, C), BF16), dma((5,))],
        60, "start", loose=(ocean_state.transpose(1, 2, 0), cotangent.transpose(1, 2, 0), land_mask),
    )
    halo = swap(outer, lat, False)
    halo_in = swap(inner, lat, True)
    inner2, pre_o, dact_o, fold1, spread1 = call(
        first_kernel, (flags, fold_partner), (outer, inner, halo_in, mask_i, conv_first, conv_second), [pair],
        near_s + [wide_s, wide_s, pltpu.VMEM((n, ROW), F32), pltpu.VMEM((n, ROW), F32), row_s, dma((2,))], 60, "first",
        loose_outs=[wide, wide, row, taps1],
    )
    outer2 = call(
        far_kernel, (flags,), ((halo, 0), conv_first, pre_o, mask_o, (halo, 1), conv_second, dact_o), [pair],
        far_s, 60, "far", loose=(fold1, spread1),
    )[0]
    halo2 = swap(outer2, lat, False)
    halo_in2 = swap(inner2, lat, True)
    keep, give, spread2, own1, own2, *blank = call(
        weights_kernel, (flags, fold_partner), (outer, inner, halo_in, (halo, 0), (halo, 1), outer2, inner2), [part, part],
        [pltpu.VMEM((9, C, C), F32)] * 2 + [pltpu.VMEM((n, 3 * ROW), BF16)] * 2
        + [pltpu.VMEM((n, ROW), BF16)] * 2 + [row_s, dma((2,)), wide_s, wide_s], 60, "wgrad",
        loose=(fold1, spread1, conv_first), loose_outs=[wide, own, own, row, wide, row, wide, row],
    )

    def body(carry):
        turn, given, _ = carry
        now = flags + 2 * turn
        arrived = swap(given, lat, True)
        kept, taken = keep, arrived
        params = pltpu.CompilerParams(vmem_limit_bytes=8 * MiB)
        cost = pl.CostEstimate(flops=1000, transcendentals=0, bytes_accessed=1000)
        left = list(range(bits - 1, 0, -1))
        beside = []
        for stage, bit in enumerate(order):
            axis = left.index(bit)
            split = (2**axis, 2, 2 ** (len(left) - axis - 1) * 2, per, C)
            left.pop(axis)
            half = jax.ShapeDtypeStruct(split[:1] + split[2:], F32)
            sent = jax.ShapeDtypeStruct(half.shape, LINKS.get(stage, F32))
            go, kept = pl.pallas_call(
                functools.partial(halve_kernel, 2 + stage), in_specs=[SMEM, VMEM, VMEM], out_specs=(VMEM, VMEM),
                out_shape=(sent, half), compiler_params=params, cost_estimate=cost, name=f"halve{stage}",
            )(now, kept.reshape(split), taken.reshape(split))
            if 1 <= stage <= 2:
                go, beside[stage - 1] = lax.optimization_barrier((go, beside[stage - 1]))
            pairs = [(i, i ^ (1 << bit)) for i in range(lat)]
            taken = lax.ppermute(go, "lat", pairs)
            if stage == 0:
                beside.append(
                    call(
                        second_forward_kernel, (now, fold_partner),
                        ((outer2, 0), (inner2, 0), (halo_in2, 0), conv_second, (outer, 0), (inner, 0), mask_i), [row, wide],
                        near_s[0:1] + near_s[2:3] + near_s[4:5] + [wide_s, wide_s, row_s], 30, "second", loose_outs=[row],
                    )
                )
                beside.append(
                    call(
                        second_adjoint_kernel, (now,),
                        ((outer2, 1), (inner2, 1), (halo_in2, 1), conv_first, (outer, 1), (inner, 1)), [row, wide],
                        near_s[0:1] + near_s[3:4] + near_s[4:5], 28, "second_adjoint",
                    )
                )
        total = pl.pallas_call(
            total_kernel, in_specs=[VMEM, VMEM], out_specs=(VMEM, VMEM), out_shape=(own, own), compiler_params=params,
            cost_estimate=cost, name="total",
        )(kept.reshape(2, per, C), taken.reshape(2, per, C))
        return turn + 1, arrived, (list(total), beside)

    stop = jnp.minimum(1, parity + 1)
    start = ([own1, own2], [[blank[0], blank[1], blank[4]], [blank[2], blank[3]]])
    _, _, ((g1, g2), (near, near_a)) = lax.while_loop(lambda c: c[0] < stop, body, (jnp.int32(0), give, start))
    fold2 = near[2], spread2
    (upd_i, upd_o), (grad_i, grad_o) = near[:2], near_a[:2]
    updated, grad = call(
        last_kernel, (flags,), ((halo2, 0), conv_second, upd_o, mask_o, (halo2, 1), conv_first, grad_o, upd_i, grad_i), [],
        [pltpu.VMEM((n, ROW), BF16)] * 2 + [wide_s] * 2 + [row_s, dma((2,)), row_s, row_s, dma((4,))], 28, "last", loose=tuple(fold2), loose_outs=[pair, pair],
    )
    return (updated.transpose(2, 0, 1), grad.transpose(2, 0, 1), g1, g2)


def solution(mesh):
    placed = (
        P(None, ("rep", "lat"), None),
        P(None, ("rep", "lat"), None),
        P("lat", None),
        P(),
        P(),
        P(),
    )
    return jax.shard_map(
        on_device,
        mesh=mesh,
        in_specs=placed,
        out_specs=(
            P(None, ("rep", "lat"), None),
            P(None, ("rep", "lat"), None),
            P(("rep", "lat"), None),
            P(("rep", "lat"), None),
        ),
        check_vma=False,
    )
```
